32 devices in a mesh: ctx: 8 (over y, x, core), tp: 4 (over z).
Axes of the slice: x: 2, y: 2, z: 4, core: 2. Of those that a mesh axis runs over, the one named last changes fastest.
Arguments:
- layer_input: bfloat16 [4096, 1024], P(('ctx', 'tp')), may hold values from -6 to 6
- out_cotangent: bfloat16 [4096, 1024], P(('ctx', 'tp')), may hold values from -6 to 6
- block_map: int32 [8], replicated, may hold values from 0 to 7, each once
- first_gain: float32 [1024], replicated, may hold values from 0.5 to 1.5
- query_weight: bfloat16 [1024, 2048], P(None, 'tp'), may hold values from -0.1875 to 0.1875
- key_weight: bfloat16 [1024, 1024], P(None, 'tp'), may hold values from -0.1875 to 0.1875
- value_weight: bfloat16 [1024, 1024], P(None, 'tp'), may hold values from -0.1875 to 0.1875
- query_gain: float32 [128], replicated, may hold values from 0.5 to 6
- key_gain: float32 [128], replicated, may hold values from 0.5 to 6
- output_weight: bfloat16 [2048, 1024], P('tp'), may hold values from -2 to 2
- second_gain: float32 [1024], replicated, may hold values from 0.5 to 1.5
- gate_weight: bfloat16 [1024, 3072], P(None, 'tp'), may hold values from -0.1875 to 0.1875
- up_weight: bfloat16 [1024, 3072], P(None, 'tp'), may hold values from -0.1875 to 0.1875
- down_weight: bfloat16 [3072, 1024], P('tp'), may hold values from -0.109375 to 0.109375
Outputs:
- layer_output: float32 [4096, 1024], P(('ctx', 'tp'))
- input_grad: float32 [4096, 1024], P(('ctx', 'tp'))
- first_gain_grad: float32 [1024], replicated
- query_weight_grad: float32 [1024, 2048], P('ctx', 'tp')
- key_weight_grad: float32 [1024, 1024], P('ctx', 'tp')
- value_weight_grad: float32 [1024, 1024], P('ctx', 'tp')
- query_gain_grad: float32 [128], replicated
- key_gain_grad: float32 [128], replicated
- output_weight_grad: float32 [2048, 1024], P('tp', 'ctx')
- second_gain_grad: float32 [1024], replicated
- gate_weight_grad: float32 [1024, 3072], P('ctx', 'tp')
- up_weight_grad: float32 [1024, 3072], P('ctx', 'tp')
- down_weight_grad: float32 [3072, 1024], P('tp', 'ctx')
The draws below stay inside these ranges and needn't reach their ends.
Inputs may be any that keep to these rules, and one draw needn't show every extreme that they name: block_map names each of 0 to 7 once.
All inputs are finite; a program needn't handle non-finite values.
Results may differ from the reference program's by a relative error of at most 0.034.
The reference program's roundings to bfloat16 on the way count: a program that leaves them out, or rounds other values in their place, can miss the bound.
Values may be sent and summed in bfloat16 or wider, within the bound.
No kernel may reach another device: no remote copies, remote signals or barrier semaphores. Data moves between devices by JAX's collectives and lax.ppermute only.
A program may use at most 192 MiB of HBM per device.

```python
import math
import jax
import jax.numpy as jnp
from jax import lax

D = 1024
H = 16
KV = 8
HD = 128
FF = 3072
BLK = 256
SEQ = 4096
N_CTX = 8


def head_gain(key, salt):
    folded = jax.random.fold_in(key, salt)
    return jax.random.uniform(folded, (HD,), jnp.float32, 0.5, 1.5)


def draw_query_gain(key, part):
    return head_gain(key, 11)


def draw_key_gain(key, part):
    return head_gain(key, 23)


def shard_levels(rng, dims, shards, smallest, high):
    def one(dim, blocks):
        steps = jax.random.uniform(jax.random.fold_in(jax.random.fold_in(rng, 6), dim), (blocks,), jnp.float32, smallest / len(shards), high / len(shards))
        return jnp.repeat(jnp.exp(steps), dims[dim] // blocks).reshape((-1,) + (1,) * (len(dims) - dim - 1))

    gain = one(*shards[0])
    for cut in shards[1:]:
        gain = gain * one(*cut)
    return gain


def noise(rng, extent, spread, limit, cuts=(), held_as=jnp.bfloat16):
    entries = spread * jax.random.normal(rng, extent, jnp.float32)
    if cuts:
        entries = entries * shard_levels(rng, extent, cuts, -0.22, 0.18)
    return jnp.clip(entries, -limit, limit).astype(held_as)


def setup_inputs(seed: int = 0) -> dict:
    key_list = jax.random.split(jax.random.key(seed), 15)
    return {
        "layer_input": noise(key_list[0], (SEQ, D), 1.0, 6.0, ((0, 32),)),
        "out_cotangent": noise(key_list[1], (SEQ, D), 1.0, 6.0, ((0, 32),)),
        "block_map": jax.random.permutation(key_list[2], N_CTX).astype(jnp.int32),
        "first_gain": jnp.clip(1.0 + 0.1 * jax.random.normal(key_list[3], (D,), jnp.float32), 0.5, 1.5),
        "query_weight": noise(key_list[4], (D, H * HD), D ** -0.5, 0.1875, ((1, 4),)),
        "key_weight": noise(key_list[5], (D, KV * HD), D ** -0.5, 0.1875, ((1, 4),)),
        "value_weight": noise(key_list[6], (D, KV * HD), D ** -0.5, 0.1875, ((1, 4),)),
        "query_gain": draw_query_gain(jax.random.fold_in(key_list[14], 71), 0),
        "key_gain": draw_key_gain(jax.random.fold_in(key_list[14], 71), 0),
        "output_weight": noise(key_list[9], (H * HD, D), 8 ** -0.5, 2.0, ((0, 4),)),
        "second_gain": jnp.clip(1.0 + 0.1 * jax.random.normal(key_list[10], (D,), jnp.float32), 0.5, 1.5),
        "gate_weight": noise(key_list[11], (D, FF), D ** -0.5, 0.1875, ((1, 4),)),
        "up_weight": noise(key_list[12], (D, FF), D ** -0.5, 0.1875, ((1, 4),)),
        "down_weight": noise(key_list[13], (FF, D), FF ** -0.5, 0.109375, ((0, 4),)),
    }


EPSILON = 1e-06
ROPE_BASE = 1000000.0
NEGATIVE = -1e+30

def rms_apply(values, scaling):
    factor = lax.rsqrt(lax.optimization_barrier(jnp.mean(values * values, axis=-1, keepdims=True)) + EPSILON)
    return values * factor * scaling

def rotate_half(values):
    half_dim = values.shape[-1] // 2
    return jnp.concatenate([-values[..., half_dim:], values[..., :half_dim]], axis=-1)

def head_transform(linear, scaling, cosine_table, sine_table):
    normed = rms_apply(linear, scaling)
    return normed * cosine_table + rotate_half(normed) * sine_table

def rope_tables(positions, head_dim):
    half_dim = head_dim // 2
    inverse = jnp.exp(jnp.arange(half_dim).astype(jnp.float32) * (-2.0 * math.log(ROPE_BASE) / head_dim))
    angles = positions.astype(jnp.float32)[:, None] * inverse[None, :]
    cosine_table = jnp.concatenate([jnp.cos(angles), jnp.cos(angles)], axis=-1)[:, None, :]
    sine_table = jnp.concatenate([jnp.sin(angles), jnp.sin(angles)], axis=-1)[:, None, :]
    return (cosine_table, sine_table)

def layout_positions(row_ids, block_map, group_rows, groups):
    group_index = row_ids // group_rows
    within = row_ids % group_rows
    block_rows = group_rows // 2
    first_block = lax.optimization_barrier(jnp.sum(jnp.where(group_index[:, None] == jnp.arange(groups, dtype=jnp.int32)[None, :], block_map[None, :], 0), axis=1))
    block_index = jnp.where(within < block_rows, first_block, 2 * groups - 1 - first_block)
    return (block_index * block_rows + within % block_rows).astype(jnp.int32)

def rounded(values):
    return lax.optimization_barrier(values.astype(jnp.bfloat16)).astype(jnp.float32)

def reference(layer_input, out_cotangent, block_map, first_gain, query_weight, key_weight, value_weight, query_gain, key_gain, output_weight, second_gain, gate_weight, up_weight, down_weight):
    repeat = H // KV
    score_scale = 1.0 / math.sqrt(HD)
    positions = layout_positions(jnp.arange(SEQ, dtype=jnp.int32), block_map, 2 * BLK, N_CTX)
    cosine_table, sine_table = rope_tables(positions, HD)

    def query_side(linear, scaling):
        return head_transform(linear, scaling, cosine_table, sine_table)
    inputs_float = layer_input.astype(jnp.float32)
    normed_a = rms_apply(inputs_float, first_gain).astype(jnp.bfloat16)
    query_linear = jnp.dot(normed_a, query_weight, preferred_element_type=jnp.float32).reshape(SEQ, H, HD)
    key_linear = jnp.dot(normed_a, key_weight, preferred_element_type=jnp.float32).reshape(SEQ, KV, HD)
    values = jnp.dot(normed_a, value_weight, preferred_element_type=jnp.float32).astype(jnp.bfloat16).reshape(SEQ, KV, HD)
    query_rot, query_pull = jax.vjp(query_side, query_linear, query_gain)
    key_rot, key_pull = jax.vjp(query_side, key_linear, key_gain)
    queries = query_rot.astype(jnp.bfloat16)
    keys = key_rot.astype(jnp.bfloat16)
    keys_float = keys.astype(jnp.float32)
    values_float = values.astype(jnp.float32)
    block_size = math.gcd(SEQ, 512)
    blocks = SEQ // block_size
    query_blocks = queries.reshape(blocks, block_size, KV, repeat, HD)
    query_positions = positions.reshape(blocks, block_size)

    def forward_block(operands):
        block_queries, block_pos = operands
        scores = jnp.einsum('qgrd,kgd->grqk', block_queries.astype(jnp.float32), keys_float) * score_scale
        allowed = positions[None, None, None, :] <= block_pos[None, None, :, None]
        scores = jnp.where(allowed, scores, NEGATIVE)
        row_max = lax.optimization_barrier(jnp.max(scores, axis=-1))
        weights = jnp.where(allowed, jnp.exp(scores - row_max[..., None]), 0.0)
        row_sum = lax.optimization_barrier(jnp.sum(weights, axis=-1))
        mixed = jnp.einsum('grqk,kgd->qgrd', rounded(weights), values_float)
        block_out = (mixed / jnp.transpose(row_sum, (2, 0, 1))[..., None]).astype(jnp.bfloat16)
        return (block_out, row_max + jnp.log(row_sum))
    attended_blocks, log_total = lax.map(forward_block, (query_blocks, query_positions))
    attended = attended_blocks.reshape(SEQ, H * HD)
    residual = inputs_float + jnp.dot(attended, output_weight, preferred_element_type=jnp.float32)
    normed_b = rms_apply(residual, second_gain).astype(jnp.bfloat16)
    gate = jnp.dot(normed_b, gate_weight, preferred_element_type=jnp.float32)
    upward = jnp.dot(normed_b, up_weight, preferred_element_type=jnp.float32)
    sigmoid_gate = jax.nn.sigmoid(gate)
    hidden = (gate * sigmoid_gate * upward).astype(jnp.bfloat16)
    layer_output = residual + jnp.dot(hidden, down_weight, preferred_element_type=jnp.float32)
    d_hidden = jnp.dot(out_cotangent, down_weight.T, preferred_element_type=jnp.float32)
    d_gate = (d_hidden * upward * sigmoid_gate * (1.0 + gate * (1.0 - sigmoid_gate))).astype(jnp.bfloat16)
    d_upward = (d_hidden * gate * sigmoid_gate).astype(jnp.bfloat16)
    gate_grad = jnp.dot(normed_b.T, d_gate, preferred_element_type=jnp.float32)
    upward_grad = jnp.dot(normed_b.T, d_upward, preferred_element_type=jnp.float32)
    down_grad = jnp.dot(hidden.T, out_cotangent, preferred_element_type=jnp.float32)
    d_second = jnp.dot(d_gate, gate_weight.T, preferred_element_type=jnp.float32) + jnp.dot(d_upward, up_weight.T, preferred_element_type=jnp.float32)
    unused_second, second_pull = jax.vjp(rms_apply, residual, second_gain)
    d_residual_norm, second_gain_grad = second_pull(d_second)
    d_residual = out_cotangent.astype(jnp.float32) + d_residual_norm
    d_residual_b = d_residual.astype(jnp.bfloat16)
    output_grad = jnp.dot(attended.T, d_residual_b, preferred_element_type=jnp.float32)
    d_attended = jnp.dot(d_residual_b, output_weight.T, preferred_element_type=jnp.float32).astype(jnp.bfloat16)
    delta = lax.optimization_barrier(jnp.sum((d_attended.astype(jnp.float32) * attended.astype(jnp.float32)).reshape(SEQ, H, HD), axis=-1))
    d_attended_blocks = d_attended.reshape(blocks, block_size, KV, repeat, HD)
    delta_blocks = delta.reshape(blocks, block_size, KV, repeat)

    def backward_block(running, operands):
        key_acc, value_acc = running
        block_queries, block_pos, block_lse, block_d_att, block_delta = operands
        query_float = block_queries.astype(jnp.float32)
        d_att_float = block_d_att.astype(jnp.float32)
        scores = jnp.einsum('qgrd,kgd->grqk', query_float, keys_float) * score_scale
        allowed = positions[None, None, None, :] <= block_pos[None, None, :, None]
        probs = jnp.where(allowed, jnp.exp(jnp.where(allowed, scores, NEGATIVE) - block_lse[..., None]), 0.0)
        value_acc = value_acc + jnp.einsum('grqk,qgrd->kgd', rounded(probs), d_att_float)
        d_probs = jnp.einsum('qgrd,kgd->grqk', d_att_float, values_float)
        d_scores = rounded(probs * (d_probs - jnp.transpose(block_delta, (1, 2, 0))[..., None]))
        block_d_queries = jnp.einsum('grqk,kgd->qgrd', d_scores, keys_float) * score_scale
        key_acc = key_acc + jnp.einsum('grqk,qgrd->kgd', d_scores, query_float) * score_scale
        return ((key_acc, value_acc), block_d_queries)
    zeros_kv = jnp.zeros((SEQ, KV, HD), jnp.float32)
    (d_keys, d_values), d_query_blocks = lax.scan(backward_block, (zeros_kv, zeros_kv), (query_blocks, query_positions, log_total, d_attended_blocks, delta_blocks))
    d_queries = d_query_blocks.reshape(SEQ, H, HD)
    d_query_linear, query_gain_grad = query_pull(d_queries)
    d_key_linear, key_gain_grad = key_pull(d_keys)
    d_query_b = d_query_linear.astype(jnp.bfloat16).reshape(SEQ, H * HD)
    d_key_b = d_key_linear.astype(jnp.bfloat16).reshape(SEQ, KV * HD)
    d_value_b = d_values.astype(jnp.bfloat16).reshape(SEQ, KV * HD)
    query_grad = jnp.dot(normed_a.T, d_query_b, preferred_element_type=jnp.float32)
    key_grad = jnp.dot(normed_a.T, d_key_b, preferred_element_type=jnp.float32)
    value_grad = jnp.dot(normed_a.T, d_value_b, preferred_element_type=jnp.float32)
    d_first = jnp.dot(d_query_b, query_weight.T, preferred_element_type=jnp.float32)
    d_first = d_first + jnp.dot(d_key_b, key_weight.T, preferred_element_type=jnp.float32)
    d_first = d_first + jnp.dot(d_value_b, value_weight.T, preferred_element_type=jnp.float32)
    unused_first, first_pull = jax.vjp(rms_apply, inputs_float, first_gain)
    d_input_norm, first_gain_grad = first_pull(d_first)
    input_grad = d_residual + d_input_norm
    return (layer_output, input_grad, first_gain_grad, query_grad, key_grad, value_grad, query_gain_grad, key_gain_grad, output_grad, second_gain_grad, gate_grad, upward_grad, down_grad)
```

```python
import functools
import math

import jax
import jax.numpy as jnp
from jax import lax
from jax.experimental import pallas as pl
from jax.experimental.pallas import tpu as pltpu
from jax.sharding import PartitionSpec as P

EPSILON = 1e-06
ROPE_BASE = 1000000.0
NEGATIVE = -1e30
F32 = jnp.float32
BF16 = jnp.bfloat16
VMEM_LIMIT = 56 * 1024 * 1024


def rms_apply(values, scaling):
    factor = lax.rsqrt(jnp.mean(values * values, axis=-1, keepdims=True) + EPSILON)
    return values * factor * scaling


def rotate_half(values):
    half_dim = values.shape[-1] // 2
    return jnp.concatenate([-values[..., half_dim:], values[..., :half_dim]], axis=-1)


def head_transform(linear, scaling, cosine_table, sine_table):
    normed = rms_apply(linear, scaling)
    return normed * cosine_table + rotate_half(normed) * sine_table


def rope_tables(positions, head_dim):
    half_dim = head_dim // 2
    inverse = jnp.exp(
        jnp.arange(half_dim).astype(F32) * (-2.0 * math.log(ROPE_BASE) / head_dim)
    )
    angles = positions.astype(F32)[:, None] * inverse[None, :]
    cosine_table = jnp.concatenate([jnp.cos(angles), jnp.cos(angles)], axis=-1)[:, None, :]
    sine_table = jnp.concatenate([jnp.sin(angles), jnp.sin(angles)], axis=-1)[:, None, :]
    return (cosine_table, sine_table)


def contract_rows(left, right):
    return lax.dot_general(left, right, (((0,), (0,)), ((), ())), preferred_element_type=F32)


def project_back(left, right):
    return lax.dot_general(left, right, (((1,), (1,)), ((), ())), preferred_element_type=F32)


def dot_nn(left, right):
    return lax.dot_general(left, right, (((1,), (0,)), ((), ())), preferred_element_type=F32)


def swap(values, axis, mask):
    size = lax.axis_size(axis)
    return lax.ppermute(values, axis, [(k, k ^ mask) for k in range(size)])


def gather_slots(values, axis):
    size = lax.axis_size(axis)
    return jnp.concatenate([values] + [swap(values, axis, r) for r in range(1, size)], axis=0)


def scatter_slots(parts, axis):
    size = lax.axis_size(axis)
    rows = parts.shape[0] // size
    total = parts[:rows].astype(F32)
    for r in range(1, size):
        piece = parts[r * rows : (r + 1) * rows].astype(BF16)
        total = total + swap(piece, axis, r).astype(F32)
    return total


def gather_ctx(values, bits):
    have = {0: values}
    for bit in bits:
        mask = 1 << bit
        have.update({m ^ mask: swap(v, "ctx", mask) for m, v in have.items()})
    return [have[m] for m in sorted(have)]


def scatter_ctx(keep, send, bits):
    half = keep.shape[0]
    received = swap(send, "ctx", 1).astype(F32)
    sums = {2 * j: keep[j].astype(F32) + received[j] for j in range(half)}
    for bit in bits:
        mask = 1 << bit
        going = [m for m in sorted(sums) if m & mask]
        for m in going:
            got = swap(sums.pop(m).astype(BF16), "ctx", mask)
            sums[m ^ mask] = sums[m ^ mask] + got.astype(F32)
    return sums[0]


def reduce_weight(keep, send):
    size = lax.axis_size("ctx")
    rows = keep.shape[0] // (size // 2)
    sums = keep + swap(send.astype(BF16), "ctx", 1).astype(F32)
    total = sums[:rows]
    for j in range(1, size // 2):
        total = total + swap(sums[j * rows : (j + 1) * rows].astype(BF16), "ctx", 2 * j).astype(F32)
    return total


def sum_all(values):
    values = values + swap(values, "ctx", 1)
    for axis, masks in (
        ("ctx", range(2, lax.axis_size("ctx"), 2)),
        ("tp", range(1, lax.axis_size("tp"))),
    ):
        values = sum([swap(values, axis, m) for m in masks], values)
    return values


def start_pieces(pieces, buffers, sems):
    copies = []
    for which, refs in enumerate(pieces):
        for s, ref in enumerate(refs):
            copy = pltpu.make_async_copy(ref, buffers[which].at[s], sems.at[which, s])
            copy.start()
            copies.append((s, copy))
    return copies


def causal_mask(info_ref, half, rows):
    def order(axis):
        local = lax.broadcasted_iota(jnp.int32, (half, half), axis)
        shard = jnp.bitwise_xor(local // rows, info_ref[1])
        return shard * rows + local % rows

    return order(0) <= order(1)


def attention_forward_kernel(slots, heads, repeat, rows, *refs):
    info_ref, q_ref = refs[:2]
    k_refs = refs[2 : 2 + slots]
    v_refs = refs[2 + slots : 2 + 2 * slots]
    o_ref, lse_ref, k_buf, v_buf, m_ref, l_ref, acc_ref, sems = refs[2 + 2 * slots :]
    head_dim = acc_ref.shape[1]
    half = acc_ref.shape[2]
    scale = 1.0 / math.sqrt(head_dim)
    copies = start_pieces((k_refs, v_refs), (k_buf, v_buf), sems)
    low = pl.multiple_of(info_ref[0] * half, half)
    high = pl.multiple_of((1 - info_ref[0]) * half, half)
    own_block = info_ref[2]
    mask = causal_mask(info_ref, half, rows)

    def load_kv(s, kv, offset):
        columns = slice(kv * head_dim, (kv + 1) * head_dim)
        k = k_buf[s, pl.ds(offset, half), columns]
        v = v_buf[s, pl.ds(offset, half), columns]
        return k, v.T

    def tile(head, q_offset, k, vt, state, masked, first):
        q = q_ref[pl.ds(q_offset, half), head * head_dim : (head + 1) * head_dim]
        scores = project_back(k, q) * scale
        if masked:
            scores = jnp.where(mask, scores, NEGATIVE)
        index = state * heads + head
        peak = jnp.max(scores, axis=0, keepdims=True)
        if not first:
            old = m_ref[index]
            peak = jnp.maximum(old, peak)
        weights = jnp.exp(scores - peak)
        total = jnp.sum(weights, axis=0, keepdims=True)
        mixed = dot_nn(vt, weights.astype(BF16))
        if not first:
            fade = jnp.exp(old - peak)
            total = total + l_ref[index] * fade
            mixed = mixed + acc_ref[index] * fade
        m_ref[index] = peak
        l_ref[index] = total
        acc_ref[index] = mixed

    for s, copy in copies:
        if s == 0:
            copy.wait()
    for kv in range(heads // repeat):
        k_low, vt_low = load_kv(0, kv, low)
        k_high, vt_high = load_kv(0, kv, high)
        for head in range(kv * repeat, (kv + 1) * repeat):
            tile(head, low, k_low, vt_low, 0, True, True)
            tile(head, high, k_high, vt_high, 1, True, True)
            tile(head, high, k_low, vt_low, 2, False, True)
    for s, copy in copies:
        if s != 0:
            copy.wait()

    def step(s, carry):
        earlier = info_ref[2 + s] < own_block
        offset = pl.multiple_of(jnp.where(earlier, low, high), half)
        state = jnp.where(earlier, 0, 1)
        for kv in range(heads // repeat):
            k_low, vt_low = load_kv(s, kv, low)
            k_sel, vt_sel = load_kv(s, kv, offset)
            for head in range(kv * repeat, (kv + 1) * repeat):
                tile(head, high, k_low, vt_low, 2, False, False)
                tile(head, offset, k_sel, vt_sel, state, False, False)
        return carry

    lax.fori_loop(1, slots, step, 0)
    for head in range(heads):
        columns = slice(head * head_dim, (head + 1) * head_dim)
        o_ref[pl.ds(low, half), columns] = (acc_ref[head] / l_ref[head]).T.astype(o_ref.dtype)
        lse_ref[head] = m_ref[head] + jnp.log(l_ref[head])
        one, two = heads + head, 2 * heads + head
        peak = jnp.maximum(m_ref[one], m_ref[two])
        fade_one = jnp.exp(m_ref[one] - peak)
        fade_two = jnp.exp(m_ref[two] - peak)
        total = l_ref[one] * fade_one + l_ref[two] * fade_two
        mixed = acc_ref[one] * fade_one + acc_ref[two] * fade_two
        o_ref[pl.ds(high, half), columns] = (mixed / total).T.astype(o_ref.dtype)
        lse_ref[heads + head] = peak + jnp.log(total)


def attention_backward_kernel(slots, heads, repeat, rows, *refs):
    info_ref, q_ref, do_ref, o_ref, lse_ref = refs[:5]
    k_refs = refs[5 : 5 + slots]
    v_refs = refs[5 + slots : 5 + 2 * slots]
    (dq_ref, dk_keep, dk_send, dv_keep, dv_send, k_buf, v_buf, delta_ref, acc_ref, sems) = refs[
        5 + 2 * slots :
    ]
    head_dim = acc_ref.shape[1]
    half = acc_ref.shape[2]
    kv_heads = heads // repeat
    scale = 1.0 / math.sqrt(head_dim)
    copies = start_pieces((k_refs, v_refs), (k_buf, v_buf), sems)
    low = pl.multiple_of(info_ref[0] * half, half)
    high = pl.multiple_of((1 - info_ref[0]) * half, half)
    own_block = info_ref[2]
    mask = causal_mask(info_ref, half, rows)

    for head in range(heads):
        columns = slice(head * head_dim, (head + 1) * head_dim)
        for which, offset in ((0, low), (1, high)):
            product = do_ref[pl.ds(offset, half), columns].astype(F32) * o_ref[
                pl.ds(offset, half), columns
            ].astype(F32)
            delta_ref[which * heads + head] = jnp.sum(product.T, axis=0, keepdims=True)

    def load_kv(s, kv, offset):
        columns = slice(kv * head_dim, (kv + 1) * head_dim)
        k = k_buf[s, pl.ds(offset, half), columns]
        return k, k.T, v_buf[s, pl.ds(offset, half), columns]

    def tile(head, q_offset, loaded, which, masked, first):
        k, kt, v = loaded
        columns = slice(head * head_dim, (head + 1) * head_dim)
        q = q_ref[pl.ds(q_offset, half), columns]
        do = do_ref[pl.ds(q_offset, half), columns]
        index = which * heads + head
        probs = jnp.exp(project_back(k, q) * scale - lse_ref[index])
        if masked:
            probs = jnp.where(mask, probs, 0.0)
        d_scores = (probs * (project_back(v, do) - delta_ref[index])).astype(BF16)
        d_query = dot_nn(kt, d_scores)
        acc_ref[index] = d_query if first else acc_ref[index] + d_query
        return dot_nn(d_scores, q), dot_nn(probs.astype(BF16), do)

    def pair_sum(items):
        return sum(item[0] for item in items), sum(item[1] for item in items)

    def store(out_ref, index, offset, kv, values):
        columns = slice(kv * head_dim, (kv + 1) * head_dim)
        out_ref[index, pl.ds(offset, half), columns] = values.astype(out_ref.dtype)

    for s, copy in copies:
        if s == 0:
            copy.wait()
    for kv in range(kv_heads):
        kv_low = load_kv(0, kv, low)
        kv_high = load_kv(0, kv, high)
        on_low, on_high = [], []
        for head in range(kv * repeat, (kv + 1) * repeat):
            on_low.append(tile(head, low, kv_low, 0, True, True))
            on_high.append(tile(head, high, kv_high, 1, True, True))
            on_low.append(tile(head, high, kv_low, 1, False, False))
        dk, dv = pair_sum(on_low)
        store(dk_keep, 0, low, kv, dk * scale)
        store(dv_keep, 0, low, kv, dv)
        dk, dv = pair_sum(on_high)
        store(dk_keep, 0, high, kv, dk * scale)
        store(dv_keep, 0, high, kv, dv)
    for s, copy in copies:
        if s != 0:
            copy.wait()

    def step(s, carry):
        earlier = info_ref[2 + s] < own_block
        offset = pl.multiple_of(jnp.where(earlier, low, high), half)
        which = jnp.where(earlier, 0, 1)
        results = []
        for kv in range(kv_heads):
            kv_low = load_kv(s, kv, low)
            kv_sel = load_kv(s, kv, offset)
            on_low, on_sel = [], []
            for head in range(kv * repeat, (kv + 1) * repeat):
                on_low.append(tile(head, high, kv_low, 1, False, False))
                on_sel.append(tile(head, offset, kv_sel, which, False, False))
            dk_low, dv_low = pair_sum(on_low)
            dk_sel, dv_sel = pair_sum(on_sel)
            keep = jnp.where(earlier, 1.0, 0.0)
            results.append(
                (
                    (dk_low + dk_sel * keep) * scale,
                    dk_sel * (scale * (1.0 - keep)),
                    dv_low + dv_sel * keep,
                    dv_sel * (1.0 - keep),
                )
            )

        def write(dk_out, dv_out):
            index = lax.div(s, 2)
            for kv, (dk_low, dk_high, dv_low, dv_high) in enumerate(results):
                store(dk_out, index, low, kv, dk_low)
                store(dk_out, index, high, kv, dk_high)
                store(dv_out, index, low, kv, dv_low)
                store(dv_out, index, high, kv, dv_high)

        odd = lax.rem(s, 2) == 1
        pl.when(odd)(lambda: write(dk_send, dv_send))
        pl.when(jnp.logical_not(odd))(lambda: write(dk_keep, dv_keep))
        return carry

    lax.fori_loop(1, slots, step, 0)
    for head in range(heads):
        columns = slice(head * head_dim, (head + 1) * head_dim)
        dq_ref[pl.ds(low, half), columns] = acc_ref[head].T * scale
        dq_ref[pl.ds(high, half), columns] = acc_ref[heads + head].T * scale


VMEM_SPEC = pl.BlockSpec(memory_space=pltpu.VMEM)
ANY_SPEC = pl.BlockSpec(memory_space=pl.ANY)
SMEM_SPEC = pl.BlockSpec(memory_space=pltpu.SMEM)


def attention_forward(info, queries, keys, values, head_dim, rows):
    slots = len(keys)
    group_rows, width = queries.shape
    kv_width = keys[0].shape[1]
    heads = width // head_dim
    half = group_rows // 2
    kernel = functools.partial(
        attention_forward_kernel, slots, heads, width // kv_width, rows
    )
    return pl.pallas_call(
        kernel,
        out_shape=(
            jax.ShapeDtypeStruct((group_rows, width), BF16),
            jax.ShapeDtypeStruct((2 * heads, 1, half), F32),
        ),
        in_specs=[SMEM_SPEC, VMEM_SPEC] + [ANY_SPEC] * (2 * slots),
        out_specs=(VMEM_SPEC, VMEM_SPEC),
        scratch_shapes=[
            pltpu.VMEM((slots, group_rows, kv_width), BF16),
            pltpu.VMEM((slots, group_rows, kv_width), BF16),
            pltpu.VMEM((3 * heads, 1, half), F32),
            pltpu.VMEM((3 * heads, 1, half), F32),
            pltpu.VMEM((3 * heads, head_dim, half), F32),
            pltpu.SemaphoreType.DMA((2, slots)),
        ],
        compiler_params=pltpu.CompilerParams(vmem_limit_bytes=VMEM_LIMIT),
        name="attention_forward",
    )(info, queries, *keys, *values)


def attention_backward(info, queries, d_attended, attended, lse, keys, values, head_dim, rows):
    slots = len(keys)
    group_rows, width = queries.shape
    kv_width = keys[0].shape[1]
    heads = width // head_dim
    half = group_rows // 2
    kernel = functools.partial(
        attention_backward_kernel, slots, heads, width // kv_width, rows
    )
    piece = jax.ShapeDtypeStruct((slots // 2, group_rows, kv_width), BF16)
    return pl.pallas_call(
        kernel,
        out_shape=(jax.ShapeDtypeStruct((group_rows, width), F32), piece, piece, piece, piece),
        in_specs=[SMEM_SPEC] + [VMEM_SPEC] * 4 + [ANY_SPEC] * (2 * slots),
        out_specs=(VMEM_SPEC,) * 5,
        scratch_shapes=[
            pltpu.VMEM((slots, group_rows, kv_width), BF16),
            pltpu.VMEM((slots, group_rows, kv_width), BF16),
            pltpu.VMEM((2 * heads, 1, half), F32),
            pltpu.VMEM((2 * heads, head_dim, half), F32),
            pltpu.SemaphoreType.DMA((2, slots)),
        ],
        compiler_params=pltpu.CompilerParams(vmem_limit_bytes=VMEM_LIMIT),
        name="attention_backward",
    )(info, queries, d_attended, attended, lse, *keys, *values)


def split_slots(values, ctx_index):
    size = lax.axis_size("ctx")
    width = values.shape[1] // size
    block = lambda m: lax.dynamic_slice_in_dim(
        values, jnp.bitwise_xor(ctx_index, m) * width, width, 1
    )
    even = jnp.concatenate([block(m) for m in range(0, size, 2)], axis=1)
    odd = jnp.concatenate([block(m) for m in range(1, size, 2)], axis=1)
    return even, odd


def body(
    layer_input,
    out_cotangent,
    block_map,
    first_gain,
    query_weight,
    key_weight,
    value_weight,
    query_gain,
    key_gain,
    output_weight,
    second_gain,
    gate_weight,
    up_weight,
    down_weight,
):
    groups = lax.axis_size("ctx")
    shards = lax.axis_size("tp")
    ctx_index = lax.axis_index("ctx")
    tp_index = lax.axis_index("tp")
    bits = list(range(1, groups.bit_length() - 1))
    head_dim = query_gain.shape[0]
    query_heads = query_weight.shape[1] // head_dim
    kv_heads = key_weight.shape[1] // head_dim
    rows = layer_input.shape[0]
    group_rows = rows * shards
    half = group_rows // 2

    local = jnp.arange(group_rows, dtype=jnp.int32)
    within = jnp.bitwise_xor(local // rows, tp_index) * rows + local % rows
    own_block = lax.dynamic_index_in_dim(block_map, ctx_index, keepdims=False)
    block = jnp.where(within < half, own_block, 2 * groups - 1 - own_block)
    positions = block * half + within % half
    slot_blocks = jnp.take(block_map, jnp.bitwise_xor(jnp.arange(groups), ctx_index), axis=0)
    info = jnp.concatenate(
        [
            jnp.stack([tp_index // (shards // 2), tp_index % (shards // 2)]).astype(jnp.int32),
            slot_blocks.astype(jnp.int32),
        ]
    )

    inputs_float = layer_input.astype(F32)
    normed_first, first_pull = jax.vjp(rms_apply, inputs_float, first_gain)
    normed_a = gather_slots(normed_first.astype(BF16), "tp")
    cosine_table, sine_table = rope_tables(positions, head_dim)

    def query_side(linear, scaling):
        return head_transform(linear, scaling, cosine_table, sine_table)

    query_linear = dot_nn(normed_a, query_weight).reshape(group_rows, query_heads, head_dim)
    key_linear = dot_nn(normed_a, key_weight).reshape(group_rows, kv_heads, head_dim)
    value_rows = dot_nn(normed_a, value_weight).astype(BF16)
    query_rot, query_pull = jax.vjp(query_side, query_linear, query_gain)
    key_rot, key_pull = jax.vjp(query_side, key_linear, key_gain)
    queries = query_rot.astype(BF16).reshape(group_rows, query_heads * head_dim)
    key_rows = key_rot.astype(BF16).reshape(group_rows, kv_heads * head_dim)
    keys = gather_ctx(key_rows, bits + [0])
    values = gather_ctx(value_rows, bits[::-1] + [0])
    attended, lse = attention_forward(info, queries, keys, values, head_dim, rows)

    attention_part = scatter_slots(dot_nn(attended, output_weight), "tp")
    residual = inputs_float + attention_part
    normed_second, second_pull = jax.vjp(rms_apply, residual, second_gain)
    normed_b = gather_slots(normed_second.astype(BF16), "tp")
    cotangent_all = gather_slots(out_cotangent, "tp")
    gate = dot_nn(normed_b, gate_weight)
    upward = dot_nn(normed_b, up_weight)
    sigmoid_gate = jax.nn.sigmoid(gate)
    hidden = (gate * sigmoid_gate * upward).astype(BF16)
    d_hidden = project_back(cotangent_all, down_weight)
    d_gate = (d_hidden * upward * sigmoid_gate * (1.0 + gate * (1.0 - sigmoid_gate))).astype(BF16)
    d_upward = (d_hidden * gate * sigmoid_gate).astype(BF16)
    d_second = scatter_slots(
        project_back(d_gate, gate_weight) + project_back(d_upward, up_weight), "tp"
    )
    d_residual_norm, second_gain_part = second_pull(d_second)
    d_residual = out_cotangent.astype(F32) + d_residual_norm
    d_residual_all = gather_slots(d_residual.astype(BF16), "tp")
    feedforward_part = scatter_slots(dot_nn(hidden, down_weight), "tp")
    layer_output = residual + feedforward_part

    normed_even, normed_odd = split_slots(normed_b, ctx_index)
    cot_even, cot_odd = split_slots(cotangent_all, ctx_index)
    gate_sum = reduce_weight(contract_rows(normed_even, d_gate), contract_rows(normed_odd, d_gate))
    upward_sum = reduce_weight(
        contract_rows(normed_even, d_upward), contract_rows(normed_odd, d_upward)
    )
    down_sum = reduce_weight(contract_rows(cot_even, hidden), contract_rows(cot_odd, hidden))

    d_attended = project_back(d_residual_all, output_weight).astype(BF16)
    dq, dk_keep, dk_send, dv_keep, dv_send = attention_backward(
        info, queries, d_attended, attended, lse, keys, values, head_dim, rows
    )
    res_even, res_odd = split_slots(d_residual_all, ctx_index)
    output_sum = reduce_weight(contract_rows(res_even, attended), contract_rows(res_odd, attended))
    d_key_rows = scatter_ctx(dk_keep, dk_send, bits)
    d_value_rows = scatter_ctx(dv_keep, dv_send, bits[::-1])
    d_query_linear, query_gain_part = query_pull(dq.reshape(group_rows, query_heads, head_dim))
    d_key_linear, key_gain_part = key_pull(d_key_rows.reshape(group_rows, kv_heads, head_dim))
    d_query_b = d_query_linear.astype(BF16).reshape(group_rows, query_heads * head_dim)
    d_key_b = d_key_linear.astype(BF16).reshape(group_rows, kv_heads * head_dim)
    d_value_b = d_value_rows.astype(BF16)
    total_term = project_back(d_query_b, query_weight)
    total_term = total_term + project_back(d_key_b, key_weight)
    d_first = scatter_slots(total_term + project_back(d_value_b, value_weight), "tp")
    first_even, first_odd = split_slots(normed_a, ctx_index)
    query_sum = reduce_weight(
        contract_rows(first_even, d_query_b), contract_rows(first_odd, d_query_b)
    )
    key_sum = reduce_weight(contract_rows(first_even, d_key_b), contract_rows(first_odd, d_key_b))
    value_sum = reduce_weight(
        contract_rows(first_even, d_value_b), contract_rows(first_odd, d_value_b)
    )
    d_input_norm, first_gain_part = first_pull(d_first)
    input_grad = d_residual + d_input_norm
    gains = sum_all(
        jnp.concatenate([first_gain_part, second_gain_part, query_gain_part, key_gain_part])
    )
    width = first_gain.shape[0]
    return (
        layer_output,
        input_grad,
        gains[:width],
        query_sum,
        key_sum,
        value_sum,
        gains[2 * width : 2 * width + head_dim],
        gains[2 * width + head_dim :],
        output_sum.T,
        gains[width : 2 * width],
        gate_sum,
        upward_sum,
        down_sum.T,
    )


def solution(mesh):
    return jax.shard_map(
        body,
        mesh=mesh,
        in_specs=(
            P(("ctx", "tp"), None),
            P(("ctx", "tp"), None),
            P(),
            P(),
            P(None, "tp"),
            P(None, "tp"),
            P(None, "tp"),
            P(),
            P(),
            P("tp", None),
            P(),
            P(None, "tp"),
            P(None, "tp"),
            P("tp", None),
        ),
        out_specs=(
            P(("ctx", "tp"), None),
            P(("ctx", "tp"), None),
            P(),
            P("ctx", "tp"),
            P("ctx", "tp"),
            P("ctx", "tp"),
            P(),
            P(),
            P("tp", "ctx"),
            P(),
            P("ctx", "tp"),
            P("ctx", "tp"),
            P("tp", "ctx"),
        ),
        check_vma=False,
    )
```

```python
import functools
import math

import jax
import jax.numpy as jnp
from jax import lax
from jax.experimental import pallas as pl
from jax.experimental.pallas import tpu as pltpu
from jax.sharding import PartitionSpec as P


EPSILON = 1e-06
ROPE_BASE = 1000000.0
NEGATIVE = -1e30
F32 = jnp.float32
BF16 = jnp.bfloat16
VMEM_LIMIT = 56 * 1024 * 1024


def rms_apply(values, scaling):
    factor = lax.rsqrt(jnp.mean(values * values, axis=-1, keepdims=True) + EPSILON)
    return values * factor * scaling


def rope_tables(positions, head_dim):
    half_dim = head_dim // 2
    inverse = jnp.exp(
        jnp.arange(half_dim).astype(F32) * (-2.0 * math.log(ROPE_BASE) / head_dim)
    )
    angles = positions.astype(F32)[:, None] * inverse[None, :]
    cosine, sine = jnp.cos(angles), jnp.sin(angles)
    cosine_table = jnp.concatenate([cosine, cosine], axis=-1)
    signed_sine_table = jnp.concatenate([-sine, sine], axis=-1)
    return (cosine_table, signed_sine_table)


def contract_rows(left, right):
    return lax.dot_general(left, right, (((0,), (0,)), ((), ())), preferred_element_type=F32)


def project_back(left, right):
    return lax.dot_general(left, right, (((1,), (1,)), ((), ())), preferred_element_type=F32)


def dot_nn(left, right):
    return lax.dot_general(left, right, (((1,), (0,)), ((), ())), preferred_element_type=F32)


def swap(values, axis, mask):
    size = lax.axis_size(axis)
    return lax.ppermute(values, axis, [(k, k ^ mask) for k in range(size)])


def after(values, *others):
    return lax.optimization_barrier((values,) + others)[0]


def gather_slots(values, axis):
    return [values] + [swap(values, axis, r) for r in range(1, lax.axis_size(axis))]


def scatter_slots(parts, axis):
    pieces = [swap(part, axis, r) for r, part in enumerate(parts) if r]
    return sum([piece.astype(F32) for piece in pieces], parts[0].astype(F32))


def gather_ctx(keys, values, bits):
    streams = [{0: keys}, {0: values}]
    for stage in range(len(bits) + 1):
        for have, order in zip(streams, (bits + [0], bits[::-1] + [0])):
            mask = 1 << order[stage]
            have.update({m ^ mask: swap(v, "ctx", mask) for m, v in have.items()})
    return [[have[m] for m in sorted(have)] for have in streams]


def exchange_ctx(keep, send):
    received = swap(send, "ctx", 1)
    own, *going = core_sum(keep, received, lax.axis_size("ctx") // 2)
    return own, [swap(part, "ctx", 2 * (j + 1)) for j, part in enumerate(going)]


def total_of(own, pieces):
    return sum([piece.astype(F32) for piece in pieces], own)


def sum_all(values):
    values = values + swap(values, "ctx", 1)
    for axis, masks in (
        ("ctx", range(2, lax.axis_size("ctx"), 2)),
        ("tp", range(1, lax.axis_size("tp"))),
    ):
        values = sum([swap(values, axis, m) for m in masks], values)
    return values


VMEM_SPEC = pl.BlockSpec(memory_space=pltpu.VMEM)
ANY_SPEC = pl.BlockSpec(memory_space=pl.ANY)
SMEM_SPEC = pl.BlockSpec(memory_space=pltpu.SMEM)
PARAMS = pltpu.CompilerParams(vmem_limit_bytes=VMEM_LIMIT)
LOG2E = math.log2(math.e)


def shape(dims, dtype):
    return jax.ShapeDtypeStruct(tuple(dims), dtype)


def rotate_lanes(values):
    return pltpu.roll(values, values.shape[-1] // 2, axis=values.ndim - 1)


def head_forward(linear, gain, cosine, sine):
    factor = lax.rsqrt(jnp.mean(linear * linear, axis=-1, keepdims=True) + EPSILON)
    normed = linear * factor * gain
    return normed * cosine + rotate_lanes(normed) * sine


def key_value_kernel(size, *refs):
    x_refs = refs[:size]
    gain, key_w, value_w, key_gain, cosine, sine = refs[size : size + 6]
    normed_ref, linear_ref, key_ref, value_ref = refs[size + 6 :]
    rows = x_refs[0].shape[0]
    head_dim = key_gain.shape[1]
    for r in range(size):
        span = slice(r * rows, (r + 1) * rows)
        x = x_refs[r][...].astype(F32)
        factor = lax.rsqrt(jnp.mean(x * x, axis=-1, keepdims=True) + EPSILON)
        normed = (x * factor * gain[...]).astype(BF16)
        normed_ref[span, :] = normed
        linear = dot_nn(normed, key_w[...])
        linear_ref[span, :] = linear
        for h in range(linear.shape[1] // head_dim):
            columns = slice(h * head_dim, (h + 1) * head_dim)
            key_ref[span, columns] = head_forward(
                linear[:, columns], key_gain[...], cosine[span, :], sine[span, :]
            ).astype(BF16)
        value_ref[span, :] = dot_nn(normed, value_w[...]).astype(BF16)


def key_value(x_slots, gain, key_weight, value_weight, key_gain, cosine, sine):
    size = len(x_slots)
    group_rows = size * x_slots[0].shape[0]
    width = key_weight.shape[1]
    return pl.pallas_call(
        functools.partial(key_value_kernel, size),
        out_shape=(
            shape((group_rows, x_slots[0].shape[1]), BF16),
            shape((group_rows, width), F32),
            shape((group_rows, width), BF16),
            shape((group_rows, width), BF16),
        ),
        in_specs=[VMEM_SPEC] * (size + 6),
        out_specs=(VMEM_SPEC,) * 4,
        compiler_params=PARAMS,
        name="key_value",
    )(*x_slots, gain[None], key_weight, value_weight, key_gain[None], cosine, sine)


def query_kernel(normed_ref, weight_ref, gain, cosine, sine, linear_ref, query_ref):
    head_dim = gain.shape[1]
    chunk = min(256, normed_ref.shape[0])
    for start in range(0, normed_ref.shape[0], chunk):
        span = slice(start, start + chunk)
        linear = dot_nn(normed_ref[span, :], weight_ref[...])
        linear_ref[span, :] = linear
        for h in range(linear.shape[1] // head_dim):
            columns = slice(h * head_dim, (h + 1) * head_dim)
            query_ref[span, columns] = head_forward(
                linear[:, columns], gain[...], cosine[span, :], sine[span, :]
            ).astype(BF16)


def query_side(normed, weight, gain, cosine, sine):
    dims = (normed.shape[0], weight.shape[1])
    return pl.pallas_call(
        query_kernel,
        out_shape=(shape(dims, F32), shape(dims, BF16)),
        in_specs=[VMEM_SPEC] * 5,
        out_specs=(VMEM_SPEC,) * 2,
        compiler_params=PARAMS,
        name="query_side",
    )(normed, weight, gain[None], cosine, sine)


def head_backward(d, linear, gain, cosine, sine):
    d = d * cosine - rotate_lanes(d) * sine
    factor = lax.rsqrt(jnp.mean(linear * linear, axis=-1, keepdims=True) + EPSILON)
    unit = linear * factor
    gain_part = jnp.sum(d * unit, axis=0, keepdims=True)
    d = d * gain
    inner = jnp.mean(d * unit, axis=-1, keepdims=True)
    return (d - unit * inner) * factor, gain_part


def query_backward_kernel(d_ref, linear_ref, weight, gain, cosine, sine, out_ref, term_ref, gain_ref):
    head_dim = gain.shape[1]
    chunk = min(256, d_ref.shape[0])
    total = jnp.zeros((1, head_dim), F32)
    for start in range(0, d_ref.shape[0], chunk):
        span = slice(start, start + chunk)
        for h in range(d_ref.shape[1] // head_dim):
            columns = slice(h * head_dim, (h + 1) * head_dim)
            d, part = head_backward(
                d_ref[span, columns],
                linear_ref[span, columns],
                gain[...],
                cosine[span, :],
                sine[span, :],
            )
            total = total + part
            out_ref[span, columns] = d.astype(BF16)
        term_ref[span, :] = project_back(out_ref[span, :], weight[...])
    gain_ref[...] = total


def query_backward(d, linear, weight, gain, cosine, sine):
    return pl.pallas_call(
        query_backward_kernel,
        out_shape=(
            shape(d.shape, BF16),
            shape((d.shape[0], weight.shape[0]), F32),
            shape((1, gain.shape[0]), F32),
        ),
        in_specs=[VMEM_SPEC] * 6,
        out_specs=(VMEM_SPEC,) * 3,
        compiler_params=PARAMS,
        name="query_backward",
    )(d, linear, weight, gain[None], cosine, sine)


def first_kernel(pieces, shards, *refs):
    own_ref, got = refs[0], refs[1 : 1 + pieces]
    linear_ref, key_w, value_w, gain, cosine, sine, term_ref, normed_ref = refs[
        1 + pieces : 9 + pieces
    ]
    dk_ref, dv_ref, gain_ref, first_ref, *part_refs = refs[9 + pieces :]
    head_dim = gain.shape[1]
    width = linear_ref.shape[1]
    rows = own_ref.shape[0] // shards
    total = jnp.zeros((1, head_dim), F32)
    first = jnp.zeros((1, normed_ref.shape[1]), F32)
    for r in range(shards):
        span = slice(r * rows, (r + 1) * rows)
        both = own_ref[span, :]
        for ref in got:
            both = both + ref[span, :].astype(F32)
        for h in range(width // head_dim):
            columns = slice(h * head_dim, (h + 1) * head_dim)
            d, part = head_backward(
                both[:, columns],
                linear_ref[span, columns],
                gain[...],
                cosine[span, :],
                sine[span, :],
            )
            total = total + part
            dk_ref[span, columns] = d.astype(BF16)
        dv_ref[span, :] = both[:, width:].astype(BF16)
        term = term_ref[span, :] + project_back(dk_ref[span, :], key_w[...])
        term = term + project_back(dv_ref[span, :], value_w[...])
        part_refs[r][...] = term.astype(part_refs[r].dtype)
        first = first + jnp.sum(term * normed_ref[span, :].astype(F32), axis=0, keepdims=True)
    gain_ref[...] = total
    first_ref[...] = first


def first_side(own, got, linear, key_weight, value_weight, gain, cosine, sine, term, normed, shards):
    model = normed.shape[1]
    part = (term.shape[0] // shards, model)
    return pl.pallas_call(
        functools.partial(first_kernel, len(got), shards),
        out_shape=(
            shape(linear.shape, BF16),
            shape(linear.shape, BF16),
            shape((1, gain.shape[0]), F32),
            shape((1, model), F32),
            shape(part, F32),
        )
        + (shape(part, BF16),) * (shards - 1),
        in_specs=[VMEM_SPEC] * (9 + len(got)),
        out_specs=(VMEM_SPEC,) * (4 + shards),
        compiler_params=PARAMS,
        name="first_side",
    )(own, *got, linear, key_weight, value_weight, gain[None], cosine, sine, term, normed)


def core_sum_kernel(keep_ref, got_ref, *outs):
    rows = outs[0].shape[0]
    for j, out in enumerate(outs):
        span = slice(j * rows, (j + 1) * rows)
        out[...] = (keep_ref[span, :].astype(F32) + got_ref[span, :].astype(F32)).astype(out.dtype)


def core_sum(keep, received, count):
    part = (keep.shape[0] // count, keep.shape[1])
    return pl.pallas_call(
        core_sum_kernel,
        out_shape=(shape(part, F32),) + (shape(part, BF16),) * (count - 1),
        in_specs=[VMEM_SPEC] * 2,
        out_specs=(VMEM_SPEC,) * count,
        compiler_params=PARAMS,
        name="core_sum",
    )(keep, received)


def pick_columns(ctx, lhs_ref, picked_ref, slots, parity):
    width = lhs_ref.shape[1] // slots
    lanes = max(width, 128)
    for j in range(slots // 2):
        start = jnp.bitwise_xor(ctx, 2 * j + parity) * width
        block = lhs_ref[:, pl.ds(pl.multiple_of(lax.div(start, lanes) * lanes, lanes), lanes)]
        offset = lax.rem(start, lanes)
        chosen = block[:, :width]
        for shift in range(width, lanes, width):
            chosen = jnp.where(offset == shift, block[:, shift : shift + width], chosen)
        picked_ref[:, j * width : (j + 1) * width] = chosen


def grad_kernel(slots, plan, lhs_count, rhs_count, *refs):
    ctx = refs[0][0]
    lhs = refs[1 : 1 + lhs_count]
    rhs = refs[1 + lhs_count : 1 + lhs_count + rhs_count]
    keep_ref, send_ref, picked_ref = refs[1 + lhs_count + rhs_count :]
    for parity, out in ((1, send_ref), (0, keep_ref)):
        column = 0
        for lhs_index, rhs_indices in plan:
            pick_columns(ctx, lhs[lhs_index], picked_ref, slots, parity)
            for index in rhs_indices:
                width = rhs[index].shape[1]
                out[:, column : column + width] = contract_rows(
                    picked_ref[...], rhs[index][...]
                ).astype(BF16)
                column += width


def weight_grads(ctx_index, slots, plan, lhs, rhs):
    width = sum(rhs[i].shape[1] for _, indices in plan for i in indices)
    rows, model = lhs[0].shape
    return pl.pallas_call(
        functools.partial(grad_kernel, slots, plan, len(lhs), len(rhs)),
        out_shape=(shape((model // 2, width), BF16),) * 2,
        in_specs=[SMEM_SPEC] + [VMEM_SPEC] * (len(lhs) + len(rhs)),
        out_specs=(VMEM_SPEC,) * 2,
        scratch_shapes=[pltpu.VMEM((rows, model // 2), BF16)],
        compiler_params=PARAMS,
    )(ctx_index[None], *lhs, *rhs)


def mlp_kernel(shards, *refs):
    n_refs, c_refs = refs[:shards], refs[shards : 2 * shards]
    gate_w, up_w, down_w = refs[2 * shards : 2 * shards + 3]
    outs = refs[2 * shards + 3 :]
    normed_ref, cot_ref, hidden_ref, d_gate_ref, d_up_ref = outs[:5]
    part_refs, acc_ref = outs[5:-1], outs[-1]
    rows = n_refs[0].shape[0]
    for r in range(shards):
        normed_ref[r * rows : (r + 1) * rows, :] = n_refs[r][...]
        cot_ref[r * rows : (r + 1) * rows, :] = c_refs[r][...]
    units = gate_w.shape[1]
    chunk = 256 if units % 256 == 0 else 128
    for start in range(0, units, chunk):
        span = slice(start, start + chunk)
        gate = dot_nn(normed_ref[...], gate_w[:, span])
        up = dot_nn(normed_ref[...], up_w[:, span])
        d_hidden = project_back(cot_ref[...], down_w[span, :])
        sigmoid = 1.0 / (1.0 + jnp.exp(-gate))
        swish = gate * sigmoid
        hidden_ref[:, span] = (swish * up).astype(BF16)
        d_gate = (d_hidden * up * sigmoid * (1.0 + gate * (1.0 - sigmoid))).astype(BF16)
        d_up = (d_hidden * swish).astype(BF16)
        d_gate_ref[:, span] = d_gate
        d_up_ref[:, span] = d_up
        term = project_back(d_gate, gate_w[:, span]) + project_back(d_up, up_w[:, span])
        if start:
            term = term + acc_ref[...]
        if start + chunk < units:
            acc_ref[...] = term
        else:
            for r in range(shards):
                part_refs[r][...] = term[r * rows : (r + 1) * rows].astype(part_refs[r].dtype)


def mlp_side(normed_slots, cot_slots, gate_weight, up_weight, down_weight):
    shards = len(normed_slots)
    rows, model = normed_slots[0].shape
    units = gate_weight.shape[1]
    group_rows = shards * rows
    return pl.pallas_call(
        functools.partial(mlp_kernel, shards),
        out_shape=(shape((group_rows, model), BF16),) * 2
        + (shape((group_rows, units), BF16),) * 3
        + (shape((rows, model), F32),)
        + (shape((rows, model), BF16),) * (shards - 1),
        in_specs=[VMEM_SPEC] * (2 * shards + 3),
        out_specs=(VMEM_SPEC,) * (5 + shards),
        scratch_shapes=[pltpu.VMEM((group_rows, model), F32)],
        compiler_params=PARAMS,
        name="mlp_side",
    )(*normed_slots, *cot_slots, gate_weight, up_weight, down_weight)


def feedforward_kernel(hidden_ref, weight, *part_refs):
    rows = part_refs[0].shape[0]
    for r, out in enumerate(part_refs):
        out[...] = dot_nn(hidden_ref[r * rows : (r + 1) * rows, :], weight[...]).astype(out.dtype)


def feedforward(hidden, down_weight, shards):
    part = (hidden.shape[0] // shards, down_weight.shape[1])
    return pl.pallas_call(
        feedforward_kernel,
        out_shape=(shape(part, F32),) + (shape(part, BF16),) * (shards - 1),
        in_specs=[VMEM_SPEC] * 2,
        out_specs=(VMEM_SPEC,) * shards,
        compiler_params=PARAMS,
        name="feedforward",
    )(hidden, down_weight)


def start_pieces(pieces, buffers, sems):
    copies = []
    for s in range(len(pieces[0])):
        for which, refs in enumerate(pieces):
            copy = pltpu.make_async_copy(refs[s], buffers[which].at[s], sems.at[which, s])
            copy.start()
            copies.append((s, copy))
    return copies


def wait_pieces(copies, own):
    for s, copy in copies:
        if (s == 0) == own:
            copy.wait()


def causal_mask(info_ref, half, repeat, rows):
    dims = (half, repeat * half)

    def order(axis):
        local = lax.broadcasted_iota(jnp.int32, dims, axis) % half
        shard = jnp.bitwise_xor(local // rows, info_ref[1])
        return shard * rows + local % rows

    return order(0) <= order(1)


def attention_forward_kernel(slots, shards, kv_heads, repeat, *refs):
    info_ref, q_ref, wo_ref = refs[:3]
    refs = refs[3:]
    k_refs, v_refs, refs = refs[:slots], refs[slots : 2 * slots], refs[2 * slots :]
    o_ref, lse_ref, refs = refs[0], refs[1], refs[2:]
    part_refs, refs = refs[:shards], refs[shards:]
    k_buf, v_buf, q_buf, m_a, l_a, acc_a, m_b, l_b, acc_b, sems = refs
    head_dim = acc_a.shape[1]
    half = acc_a.shape[2] // repeat
    rows = 2 * half // shards
    factor = LOG2E / math.sqrt(head_dim)
    copies = start_pieces((k_refs, v_refs), (k_buf, v_buf), sems)
    low = info_ref[0]
    high = 1 - low
    own_block = info_ref[2]
    for p in range(2):
        for kv in range(kv_heads):
            for r in range(repeat):
                column = (kv * repeat + r) * head_dim
                q_buf[p * kv_heads + kv, r * half : (r + 1) * half, :] = q_ref[
                    p * half : (p + 1) * half, column : column + head_dim
                ]

    def load_scores(s, kv, k_half, q_half):
        columns = slice(kv * head_dim, (kv + 1) * head_dim)
        span = pl.ds(pl.multiple_of(k_half * half, half), half)
        scores = project_back(k_buf[s, span, columns], q_buf[q_half * kv_heads + kv])
        return scores, v_buf[s, span, columns]

    def weigh(scores, v, old):
        peak = jnp.max(scores, axis=0, keepdims=True)
        if old is not None:
            peak = jnp.maximum(old[0], peak)
        weights = jnp.exp2((scores - peak) * factor)
        total = jnp.sum(weights, axis=0, keepdims=True)
        mixed = dot_nn(v.T, weights.astype(BF16))
        if old is not None:
            fade = jnp.exp2((old[0] - peak) * factor)
            total = total + old[1] * fade
            mixed = mixed + old[2] * fade
        return peak, total, mixed

    def save(m_ref, l_ref, acc_ref, index, state):
        m_ref[index], l_ref[index], acc_ref[index] = state

    mask = causal_mask(info_ref, half, repeat, rows)
    wait_pieces(copies, True)
    for kv in range(kv_heads):
        for p in (low, high):
            scores, v = load_scores(0, kv, p, p)
            scores = jnp.where(mask, scores, NEGATIVE)
            save(m_b, l_b, acc_b, p * kv_heads + kv, weigh(scores, v, None))
        scores, v = load_scores(0, kv, low, high)
        save(m_a, l_a, acc_a, kv, weigh(scores, v, None))
    wait_pieces(copies, False)

    def step(s, carry):
        chosen = jnp.where(info_ref[2 + s] < own_block, low, high)
        loaded = []
        for kv in range(kv_heads):
            index = chosen * kv_heads + kv
            loaded.append(
                load_scores(s, kv, low, high) + ((m_a[kv], l_a[kv], acc_a[kv]),)
            )
            loaded.append(
                load_scores(s, kv, chosen, chosen) + ((m_b[index], l_b[index], acc_b[index]),)
            )
        states = [weigh(*item) for item in loaded]
        for kv in range(kv_heads):
            save(m_a, l_a, acc_a, kv, states[2 * kv])
            save(m_b, l_b, acc_b, chosen * kv_heads + kv, states[2 * kv + 1])
        return carry

    lax.fori_loop(1, slots, step, 0)

    def finish(p, kv, peak, total, mixed):
        result = mixed / total
        lse_ref[p * kv_heads + kv] = peak * factor + jnp.log(total) * LOG2E
        span = pl.ds(pl.multiple_of(p * half, half), half)
        for r in range(repeat):
            column = (kv * repeat + r) * head_dim
            o_ref[span, column : column + head_dim] = result[
                :, r * half : (r + 1) * half
            ].T.astype(o_ref.dtype)

    for kv in range(kv_heads):
        index = low * kv_heads + kv
        finish(low, kv, m_b[index], l_b[index], acc_b[index])
        index = high * kv_heads + kv
        peak = jnp.maximum(m_a[kv], m_b[index])
        fade_a = jnp.exp2((m_a[kv] - peak) * factor)
        fade_b = jnp.exp2((m_b[index] - peak) * factor)
        finish(
            high,
            kv,
            peak,
            l_a[kv] * fade_a + l_b[index] * fade_b,
            acc_a[kv] * fade_a + acc_b[index] * fade_b,
        )
    for r in range(shards):
        part = dot_nn(o_ref[r * rows : (r + 1) * rows, :], wo_ref[...])
        part_refs[r][...] = part.astype(part_refs[r].dtype)


def attention_forward(info, queries, output_weight, keys, values, head_dim, shards):
    slots = len(keys)
    group_rows, width = queries.shape
    kv_width = keys[0].shape[1]
    kv_heads = kv_width // head_dim
    repeat = width // kv_width
    half = group_rows // 2
    model = output_weight.shape[1]
    wide = repeat * half
    part = (group_rows // shards, model)
    return pl.pallas_call(
        functools.partial(attention_forward_kernel, slots, shards, kv_heads, repeat),
        out_shape=(
            shape((group_rows, width), BF16),
            shape((2 * kv_heads, 1, wide), F32),
            shape(part, F32),
        )
        + (shape(part, BF16),) * (shards - 1),
        in_specs=[SMEM_SPEC, VMEM_SPEC, VMEM_SPEC] + [ANY_SPEC] * (2 * slots),
        out_specs=(VMEM_SPEC,) * (2 + shards),
        scratch_shapes=[
            pltpu.VMEM((slots, group_rows, kv_width), BF16),
            pltpu.VMEM((slots, group_rows, kv_width), BF16),
            pltpu.VMEM((2 * kv_heads, wide, head_dim), BF16),
            pltpu.VMEM((kv_heads, 1, wide), F32),
            pltpu.VMEM((kv_heads, 1, wide), F32),
            pltpu.VMEM((kv_heads, head_dim, wide), F32),
            pltpu.VMEM((2 * kv_heads, 1, wide), F32),
            pltpu.VMEM((2 * kv_heads, 1, wide), F32),
            pltpu.VMEM((2 * kv_heads, head_dim, wide), F32),
            pltpu.SemaphoreType.DMA((2, slots)),
        ],
        compiler_params=PARAMS,
        name="attention_forward",
    )(info, queries, output_weight, *keys, *values)


def attention_backward_kernel(slots, shards, kv_heads, repeat, *refs):
    info_ref, q_ref, o_ref, lse_ref, wo_ref = refs[:5]
    refs = refs[5:]
    g_refs, refs = refs[:shards], refs[shards:]
    k_refs, v_refs, refs = refs[:slots], refs[slots : 2 * slots], refs[2 * slots :]
    dq_ref, keep_ref, send_ref, res_ref = refs[:4]
    k_buf, v_buf, q_buf, do_buf, delta_ref, acc_a, acc_b, sems = refs[4:]
    head_dim = acc_a.shape[1]
    half = acc_a.shape[2] // repeat
    rows = 2 * half // shards
    scale = 1.0 / math.sqrt(head_dim)
    factor = LOG2E * scale
    copies = start_pieces((k_refs, v_refs), (k_buf, v_buf), sems)
    low = info_ref[0]
    high = 1 - low
    own_block = info_ref[2]
    for shard in range(shards):
        res_ref[shard * rows : (shard + 1) * rows, :] = g_refs[shard][...]
        d_attended = project_back(g_refs[shard][...], wo_ref[...]).astype(BF16)
        p, row = divmod(shard * rows, half)
        for kv in range(kv_heads):
            for r in range(repeat):
                column = (kv * repeat + r) * head_dim
                do_buf[p * kv_heads + kv, r * half + row : r * half + row + rows, :] = (
                    d_attended[:, column : column + head_dim]
                )
    for p in range(2):
        for kv in range(kv_heads):
            index = p * kv_heads + kv
            for r in range(repeat):
                column = (kv * repeat + r) * head_dim
                span = slice(r * half, (r + 1) * half)
                source = (slice(p * half, (p + 1) * half), slice(column, column + head_dim))
                q_buf[index, span, :] = q_ref[source]
                product = do_buf[index, span, :].astype(F32) * o_ref[source].astype(F32)
                delta_ref[index, :, span] = jnp.sum(product.T, axis=0, keepdims=True)

    def load(s, kv, k_half, q_half):
        columns = slice(kv * head_dim, (kv + 1) * head_dim)
        span = pl.ds(pl.multiple_of(k_half * half, half), half)
        index = q_half * kv_heads + kv
        k = k_buf[s, span, columns]
        v = v_buf[s, span, columns]
        q = q_buf[index]
        do = do_buf[index]
        return (
            project_back(k, q), project_back(v, do), k, q, do, lse_ref[index], delta_ref[index]
        )

    def unit(loaded, mask=None):
        scores, d_probs, k, q, do, lse, delta = loaded
        probs = jnp.exp2(scores * factor - lse)
        if mask is not None:
            probs = jnp.where(mask, probs, 0.0)
        d_scores = (probs * (d_probs - delta)).astype(BF16)
        d_value = dot_nn(probs.astype(BF16), do)
        return dot_nn(d_scores, q), d_value, dot_nn(k.T, d_scores)

    group = 2 * half
    kv_width = kv_heads * head_dim

    def store(out_ref, index, p, kv, d_key, d_value):
        column = kv * head_dim
        span = pl.ds(pl.multiple_of(index * group + p * half, half), half)
        out_ref[span, column : column + head_dim] = d_key.astype(BF16)
        out_ref[span, kv_width + column : kv_width + column + head_dim] = d_value.astype(BF16)

    mask = causal_mask(info_ref, half, repeat, rows)
    wait_pieces(copies, True)
    for kv in range(kv_heads):
        dk_high, dv_high, dq = unit(load(0, kv, high, high), mask)
        acc_b[high * kv_heads + kv] = dq
        store(keep_ref, 0, high, kv, dk_high * scale, dv_high)
        dk_low, dv_low, dq = unit(load(0, kv, low, low), mask)
        acc_b[low * kv_heads + kv] = dq
        dk_more, dv_more, dq = unit(load(0, kv, low, high))
        acc_a[kv] = dq
        store(keep_ref, 0, low, kv, (dk_low + dk_more) * scale, dv_low + dv_more)
    wait_pieces(copies, False)

    def step(s, carry):
        earlier = info_ref[2 + s] < own_block
        chosen = jnp.where(earlier, low, high)
        keep = jnp.where(earlier, 1.0, 0.0)
        loaded = []
        for kv in range(kv_heads):
            loaded.append(load(s, kv, low, high))
            loaded.append(load(s, kv, chosen, chosen))
        units = [unit(item) for item in loaded]
        for kv in range(kv_heads):
            index = chosen * kv_heads + kv
            dq_a, dq_b = units[2 * kv][2], units[2 * kv + 1][2]
            acc_a[kv] = acc_a[kv] + dq_a
            acc_b[index] = acc_b[index] + dq_b

        def write(out_ref):
            index = lax.div(s, 2)
            for kv in range(kv_heads):
                dk_low, dv_low, _ = units[2 * kv]
                dk_sel, dv_sel, _ = units[2 * kv + 1]
                rest = 1.0 - keep
                store(
                    out_ref, index, low, kv, (dk_low + dk_sel * keep) * scale, dv_low + dv_sel * keep
                )
                store(out_ref, index, high, kv, dk_sel * (rest * scale), dv_sel * rest)

        odd = lax.rem(s, 2) == 1
        pl.when(odd)(lambda: write(send_ref))
        pl.when(jnp.logical_not(odd))(lambda: write(keep_ref))
        return carry

    lax.fori_loop(1, slots, step, 0)

    def finish(p, kv, values):
        span = pl.ds(pl.multiple_of(p * half, half), half)
        for r in range(repeat):
            column = (kv * repeat + r) * head_dim
            dq_ref[span, column : column + head_dim] = (
                values[:, r * half : (r + 1) * half].T * scale
            )

    for kv in range(kv_heads):
        finish(low, kv, acc_b[low * kv_heads + kv])
        finish(high, kv, acc_b[high * kv_heads + kv] + acc_a[kv])


def attention_backward(
    info, queries, attended, lse, output_weight, d_residual_slots, keys, values, head_dim
):
    slots = len(keys)
    shards = len(d_residual_slots)
    group_rows, width = queries.shape
    kv_width = keys[0].shape[1]
    kv_heads = kv_width // head_dim
    repeat = width // kv_width
    half = group_rows // 2
    wide = repeat * half
    piece = shape((slots // 2 * group_rows, 2 * kv_width), BF16)
    model = output_weight.shape[1]
    return pl.pallas_call(
        functools.partial(attention_backward_kernel, slots, shards, kv_heads, repeat),
        out_shape=(
            shape((group_rows, width), F32), piece, piece, shape((group_rows, model), BF16)
        ),
        in_specs=[SMEM_SPEC] + [VMEM_SPEC] * (4 + shards) + [ANY_SPEC] * (2 * slots),
        out_specs=(VMEM_SPEC,) * 4,
        scratch_shapes=[
            pltpu.VMEM((slots, group_rows, kv_width), BF16),
            pltpu.VMEM((slots, group_rows, kv_width), BF16),
            pltpu.VMEM((2 * kv_heads, wide, head_dim), BF16),
            pltpu.VMEM((2 * kv_heads, wide, head_dim), BF16),
            pltpu.VMEM((2 * kv_heads, 1, wide), F32),
            pltpu.VMEM((kv_heads, head_dim, wide), F32),
            pltpu.VMEM((2 * kv_heads, head_dim, wide), F32),
            pltpu.SemaphoreType.DMA((2, slots)),
        ],
        compiler_params=PARAMS,
        name="attention_backward",
    )(
        info, queries, attended, lse, output_weight, *d_residual_slots, *keys, *values
    )


def body(
    layer_input,
    out_cotangent,
    block_map,
    first_gain,
    query_weight,
    key_weight,
    value_weight,
    query_gain,
    key_gain,
    output_weight,
    second_gain,
    gate_weight,
    up_weight,
    down_weight,
):
    groups = lax.axis_size("ctx")
    shards = lax.axis_size("tp")
    ctx_index = lax.axis_index("ctx")
    tp_index = lax.axis_index("tp")
    bits = list(range(1, groups.bit_length() - 1))
    head_dim = query_gain.shape[0]
    rows = layer_input.shape[0]
    group_rows = rows * shards
    half = group_rows // 2

    local = jnp.arange(group_rows, dtype=jnp.int32)
    within = jnp.bitwise_xor(local // rows, tp_index) * rows + local % rows
    own_block = lax.dynamic_index_in_dim(block_map, ctx_index, keepdims=False)
    block = jnp.where(within < half, own_block, 2 * groups - 1 - own_block)
    positions = block * half + within % half
    slot_blocks = jnp.take(block_map, jnp.bitwise_xor(jnp.arange(groups), ctx_index), axis=0)
    info = jnp.concatenate(
        [
            jnp.stack([tp_index // (shards // 2), tp_index % (shards // 2)]).astype(jnp.int32),
            slot_blocks.astype(jnp.int32),
        ]
    )

    x_slots = gather_slots(layer_input, "tp")
    cosine, sine = rope_tables(positions, head_dim)
    normed_a, key_linear, key_rows, value_rows = key_value(
        x_slots, first_gain, key_weight, value_weight, key_gain, cosine, sine
    )
    keys, values = gather_ctx(key_rows, value_rows, bits)
    cotangent_slots = gather_slots(after(out_cotangent, normed_a), "tp")
    query_linear, queries = query_side(normed_a, query_weight, query_gain, cosine, sine)
    queries, cotangent_slots = lax.optimization_barrier((queries, cotangent_slots))
    attended, lse, *attention_parts = attention_forward(
        info, queries, output_weight, keys, values, head_dim, shards
    )
    inputs_float = layer_input.astype(F32)
    residual = inputs_float + scatter_slots(attention_parts, "tp")
    normed_second, second_pull = jax.vjp(rms_apply, residual, second_gain)
    normed_slots = gather_slots(normed_second.astype(BF16), "tp")
    normed_b, cotangent_all, hidden, d_gate, d_upward, *second_parts = mlp_side(
        normed_slots, cotangent_slots, gate_weight, up_weight, down_weight
    )
    mlp_keep, mlp_send = weight_grads(
        ctx_index,
        groups,
        ((0, (0, 1)), (1, (2,))),
        (normed_b, cotangent_all),
        (d_gate, d_upward, hidden),
    )
    feedforward_parts = feedforward(hidden, down_weight, shards)
    d_second = scatter_slots(second_parts, "tp")
    mlp_own, mlp_got = exchange_ctx(mlp_keep, mlp_send)
    d_residual_norm, second_gain_part = second_pull(d_second)
    d_residual = out_cotangent.astype(F32) + d_residual_norm
    d_residual_slots = gather_slots(d_residual.astype(BF16), "tp")
    dq, dkv_keep, dkv_send, d_residual_all = attention_backward(
        info, queries, attended, lse, output_weight, d_residual_slots, keys, values, head_dim
    )
    dkv_own, dkv_got = exchange_ctx(dkv_keep, dkv_send)
    d_query_b, query_term, query_gain_part = query_backward(
        dq, query_linear, query_weight, query_gain, cosine, sine
    )
    feedforward_parts = after(tuple(feedforward_parts), dq)
    layer_output = residual + scatter_slots(feedforward_parts, "tp")
    query_keep, query_send = weight_grads(
        ctx_index, groups, ((0, (0,)), (1, (1,))), (d_residual_all, normed_a), (attended, d_query_b)
    )
    d_key_b, d_value_b, key_gain_part, first_gain_part, *first_parts = first_side(
        dkv_own,
        dkv_got,
        key_linear,
        key_weight,
        value_weight,
        key_gain,
        cosine,
        sine,
        query_term,
        normed_a,
        shards,
    )
    gains = jnp.concatenate(
        [first_gain_part[0] / first_gain, second_gain_part, query_gain_part[0], key_gain_part[0]]
    )
    d_first = scatter_slots(first_parts, "tp")
    key_keep, key_send = weight_grads(
        ctx_index, groups, ((0, (0, 1)),), (normed_a,), (d_key_b, d_value_b)
    )
    query_own, query_got = exchange_ctx(query_keep, query_send)
    key_own, key_got = exchange_ctx(key_keep, key_send)
    gains = sum_all(gains)
    first_pull = jax.vjp(lambda v: rms_apply(v, first_gain), inputs_float)[1]
    input_grad = d_residual + first_pull(d_first)[0]

    mlp_total = total_of(mlp_own, mlp_got)
    query_total = total_of(query_own, query_got)
    key_total = total_of(key_own, key_got)
    units = d_gate.shape[1]
    gate_sum, upward_sum, down_sum = (mlp_total[:, k * units : (k + 1) * units] for k in range(3))
    query_width, key_width = attended.shape[1], d_key_b.shape[1]
    output_sum, query_sum = query_total[:, :query_width], query_total[:, query_width:]
    key_sum, value_sum = key_total[:, :key_width], key_total[:, key_width:]
    width = first_gain.shape[0]
    return (
        layer_output,
        input_grad,
        gains[:width],
        query_sum,
        key_sum,
        value_sum,
        gains[2 * width : 2 * width + head_dim],
        gains[2 * width + head_dim :],
        output_sum.T,
        gains[width : 2 * width],
        gate_sum,
        upward_sum,
        down_sum.T,
    )


def solution(mesh):
    return jax.shard_map(
        body,
        mesh=mesh,
        in_specs=(
            P(("ctx", "tp"), None),
            P(("ctx", "tp"), None),
            P(),
            P(),
            P(None, "tp"),
            P(None, "tp"),
            P(None, "tp"),
            P(),
            P(),
            P("tp", None),
            P(),
            P(None, "tp"),
            P(None, "tp"),
            P("tp", None),
        ),
        out_specs=(
            P(("ctx", "tp"), None),
            P(("ctx", "tp"), None),
            P(),
            P("ctx", "tp"),
            P("ctx", "tp"),
            P("ctx", "tp"),
            P(),
            P(),
            P("tp", "ctx"),
            P(),
            P("ctx", "tp"),
            P("ctx", "tp"),
            P("tp", "ctx"),
        ),
        check_vma=False,
    )
```

```python
import functools
import math

import jax
import jax.numpy as jnp
from jax import lax
from jax.experimental import pallas as pl
from jax.experimental.pallas import tpu as pltpu
from jax.sharding import PartitionSpec as P


EPSILON = 1e-06
ROPE_BASE = 1000000.0
NEGATIVE = -1e30
F32 = jnp.float32
BF16 = jnp.bfloat16
VMEM_LIMIT = 56 * 1024 * 1024


def rms_apply(values, scaling):
    factor = lax.rsqrt(jnp.mean(values * values, axis=-1, keepdims=True) + EPSILON)
    return values * factor * scaling


def rope_tables(positions, head_dim):
    half_dim = head_dim // 2
    inverse = jnp.exp(
        jnp.arange(half_dim).astype(F32) * (-2.0 * math.log(ROPE_BASE) / head_dim)
    )
    angles = positions.astype(F32)[:, None] * inverse[None, :]
    cosine, sine = jnp.cos(angles), jnp.sin(angles)
    cosine_table = jnp.concatenate([cosine, cosine], axis=-1)
    signed_sine_table = jnp.concatenate([-sine, sine], axis=-1)
    return (cosine_table, signed_sine_table)


def contract_rows(left, right):
    return lax.dot_general(left, right, (((0,), (0,)), ((), ())), preferred_element_type=F32)


def project_back(left, right):
    return lax.dot_general(left, right, (((1,), (1,)), ((), ())), preferred_element_type=F32)


def dot_nn(left, right):
    return lax.dot_general(left, right, (((1,), (0,)), ((), ())), preferred_element_type=F32)


def swap(values, axis, mask):
    size = lax.axis_size(axis)
    return lax.ppermute(values, axis, [(k, k ^ mask) for k in range(size)])


def after(values, *others):
    return lax.optimization_barrier((values,) + others)[0]


def gather_slots(values, axis):
    have = {0: values}
    for bit in reversed(range(lax.axis_size(axis).bit_length() - 1)):
        mask = 1 << bit
        for m in sorted(have):
            have[m ^ mask] = swap(have[m], axis, mask)
    return [have[m] for m in sorted(have)]


def scatter_slots(parts, axis):
    sums = {m: part for m, part in enumerate(parts)}
    for hop, bit in enumerate(range(lax.axis_size(axis).bit_length() - 1)):
        mask = 1 << bit
        for m in sorted((m for m in sums if m & mask), reverse=True):
            going = sums.pop(m).astype(BF16)
            last = (m ^ mask) == 0
            if last and hop == 0:
                rest = {k: v for k, v in sums.items() if k}
                going, rest = lax.optimization_barrier((going, rest))
                sums.update(rest)
            got = swap(going, axis, mask)
            sums[m ^ mask] = sums[m ^ mask].astype(F32) + got.astype(F32)
    return sums[0]


def hold(values, *others):
    return lax.optimization_barrier((values, others))


def gather_ctx(keys, values, bits):
    streams = [{0: keys}, {0: values}]
    for stage in range(len(bits) + 1):
        for have, order in zip(streams, (bits + [0], bits[::-1] + [0])):
            mask = 1 << order[stage]
            have.update({m ^ mask: swap(v, "ctx", mask) for m, v in have.items()})
    return [[have[m] for m in sorted(have)] for have in streams]


def exchange_ctx(keep, send):
    received = swap(send, "ctx", 1)
    own, *going = core_sum(keep, received, lax.axis_size("ctx") // 2)
    return own, [swap(part, "ctx", 2 * (j + 1)) for j, part in enumerate(going)]


def total_of(own, pieces):
    return sum([piece.astype(F32) for piece in pieces], own)


def sum_all(values):
    values = values + swap(values, "ctx", 1)
    masks = range(2, lax.axis_size("ctx"), 2)
    values = sum([swap(values, "ctx", m) for m in masks], values)
    masks = range(1, lax.axis_size("tp"))
    return sum([swap(values, "tp", m) for m in masks], values)


VMEM_SPEC = pl.BlockSpec(memory_space=pltpu.VMEM)
ANY_SPEC = pl.BlockSpec(memory_space=pl.ANY)
SMEM_SPEC = pl.BlockSpec(memory_space=pltpu.SMEM)
PARAMS = pltpu.CompilerParams(vmem_limit_bytes=VMEM_LIMIT)
LOG2E = math.log2(math.e)


def shape(dims, dtype):
    return jax.ShapeDtypeStruct(tuple(dims), dtype)


def rotate_lanes(values):
    return pltpu.roll(values, values.shape[-1] // 2, axis=values.ndim - 1)


def head_forward(linear, gain, cosine, sine):
    factor = lax.rsqrt(jnp.mean(linear * linear, axis=-1, keepdims=True) + EPSILON)
    normed = linear * factor * gain
    return normed * cosine + rotate_lanes(normed) * sine


def key_value_kernel(size, *refs):
    x_refs = refs[:size]
    gain, key_w, value_w, key_gain, cosine, sine = refs[size : size + 6]
    normed_ref, linear_ref, key_ref, value_ref = refs[size + 6 :]
    rows = x_refs[0].shape[0]
    head_dim = key_gain.shape[1]
    for r in range(size):
        span = slice(r * rows, (r + 1) * rows)
        x = x_refs[r][...].astype(F32)
        factor = lax.rsqrt(jnp.mean(x * x, axis=-1, keepdims=True) + EPSILON)
        normed = (x * factor * gain[...]).astype(BF16)
        normed_ref[span, :] = normed
        linear = dot_nn(normed, key_w[...])
        linear_ref[span, :] = linear
        for h in range(linear.shape[1] // head_dim):
            columns = slice(h * head_dim, (h + 1) * head_dim)
            key_ref[span, columns] = head_forward(
                linear[:, columns], key_gain[...], cosine[span, :], sine[span, :]
            ).astype(BF16)
        value_ref[span, :] = dot_nn(normed, value_w[...]).astype(BF16)


def key_value(x_slots, gain, key_weight, value_weight, key_gain, cosine, sine):
    size = len(x_slots)
    group_rows = size * x_slots[0].shape[0]
    width = key_weight.shape[1]
    return pl.pallas_call(
        functools.partial(key_value_kernel, size),
        out_shape=(
            shape((group_rows, x_slots[0].shape[1]), BF16),
            shape((group_rows, width), F32),
            shape((group_rows, width), BF16),
            shape((group_rows, width), BF16),
        ),
        in_specs=[VMEM_SPEC] * (size + 6),
        out_specs=(VMEM_SPEC,) * 4,
        compiler_params=PARAMS,
        name="kv",
    )(*x_slots, gain[None], key_weight, value_weight, key_gain[None], cosine, sine)


def query_kernel(normed_ref, weight_ref, gain, cosine, sine, linear_ref, query_ref):
    head_dim = gain.shape[1]
    chunk = min(256, normed_ref.shape[0])
    for start in range(0, normed_ref.shape[0], chunk):
        span = slice(start, start + chunk)
        linear = dot_nn(normed_ref[span, :], weight_ref[...])
        linear_ref[span, :] = linear
        for h in range(linear.shape[1] // head_dim):
            columns = slice(h * head_dim, (h + 1) * head_dim)
            query_ref[span, columns] = head_forward(
                linear[:, columns], gain[...], cosine[span, :], sine[span, :]
            ).astype(BF16)


def query_side(normed, weight, gain, cosine, sine):
    dims = (normed.shape[0], weight.shape[1])
    return pl.pallas_call(
        query_kernel,
        out_shape=(shape(dims, F32), shape(dims, BF16)),
        in_specs=[VMEM_SPEC] * 5,
        out_specs=(VMEM_SPEC,) * 2,
        compiler_params=PARAMS,
        name="qs",
    )(normed, weight, gain[None], cosine, sine)


def head_backward(d, linear, gain, cosine, sine):
    d = d * cosine - rotate_lanes(d) * sine
    factor = lax.rsqrt(jnp.mean(linear * linear, axis=-1, keepdims=True) + EPSILON)
    unit = linear * factor
    gain_part = jnp.sum(d * unit, axis=0, keepdims=True)
    d = d * gain
    inner = jnp.mean(d * unit, axis=-1, keepdims=True)
    return (d - unit * inner) * factor, gain_part


def query_backward_kernel(d_ref, linear_ref, weight, gain, cosine, sine, out_ref, term_ref, gain_ref):
    head_dim = gain.shape[1]
    chunk = min(256, d_ref.shape[0])
    total = jnp.zeros((1, head_dim), F32)
    for start in range(0, d_ref.shape[0], chunk):
        span = slice(start, start + chunk)
        for h in range(d_ref.shape[1] // head_dim):
            columns = slice(h * head_dim, (h + 1) * head_dim)
            d, part = head_backward(
                d_ref[span, columns],
                linear_ref[span, columns],
                gain[...],
                cosine[span, :],
                sine[span, :],
            )
            total = total + part
            out_ref[span, columns] = d.astype(BF16)
        term_ref[span, :] = project_back(out_ref[span, :], weight[...])
    gain_ref[...] = total


def query_backward(d, linear, weight, gain, cosine, sine):
    return pl.pallas_call(
        query_backward_kernel,
        out_shape=(
            shape(d.shape, BF16),
            shape((d.shape[0], weight.shape[0]), F32),
            shape((1, gain.shape[0]), F32),
        ),
        in_specs=[VMEM_SPEC] * 6,
        out_specs=(VMEM_SPEC,) * 3,
        compiler_params=PARAMS,
        name="qb",
    )(d, linear, weight, gain[None], cosine, sine)


def first_kernel(pieces, shards, *refs):
    own_ref, got = refs[0], refs[1 : 1 + pieces]
    linear_ref, key_w, value_w, gain, cosine, sine, term_ref, normed_ref = refs[
        1 + pieces : 9 + pieces
    ]
    dk_ref, dv_ref, gain_ref, first_ref, *part_refs = refs[9 + pieces :]
    head_dim = gain.shape[1]
    width = linear_ref.shape[1]
    rows = own_ref.shape[0] // shards
    total = jnp.zeros((1, head_dim), F32)
    both = own_ref[...]
    for ref in got:
        both = both + ref[...].astype(F32)
    for h in range(width // head_dim):
        columns = slice(h * head_dim, (h + 1) * head_dim)
        d, part = head_backward(
            both[:, columns], linear_ref[:, columns], gain[...], cosine[...], sine[...]
        )
        total = total + part
        dk_ref[:, columns] = d.astype(BF16)
    dv_ref[...] = both[:, width:].astype(BF16)
    term = term_ref[...] + project_back(dk_ref[...], key_w[...])
    term = term + project_back(dv_ref[...], value_w[...])
    for r in range(shards):
        part_refs[r][...] = term[r * rows : (r + 1) * rows].astype(part_refs[r].dtype)
    gain_ref[...] = total
    first_ref[...] = jnp.sum(term * normed_ref[...].astype(F32), axis=0, keepdims=True)


def first_side(own, got, linear, key_weight, value_weight, gain, cosine, sine, term, normed, shards):
    model = normed.shape[1]
    part = (term.shape[0] // shards, model)
    return pl.pallas_call(
        functools.partial(first_kernel, len(got), shards),
        out_shape=(
            shape(linear.shape, BF16),
            shape(linear.shape, BF16),
            shape((1, gain.shape[0]), F32),
            shape((1, model), F32),
            shape(part, F32),
        )
        + (shape(part, BF16),) * (shards - 1),
        in_specs=[VMEM_SPEC] * (9 + len(got)),
        out_specs=(VMEM_SPEC,) * (4 + shards),
        compiler_params=PARAMS,
        name="fs",
    )(own, *got, linear, key_weight, value_weight, gain[None], cosine, sine, term, normed)


def core_sum_kernel(keep_ref, got_ref, *outs):
    rows = outs[0].shape[0]
    for j, out in enumerate(outs):
        span = slice(j * rows, (j + 1) * rows)
        out[...] = (keep_ref[span, :].astype(F32) + got_ref[span, :].astype(F32)).astype(out.dtype)


def core_sum(keep, received, count):
    part = (keep.shape[0] // count, keep.shape[1])
    return pl.pallas_call(
        core_sum_kernel,
        out_shape=(shape(part, F32),) + (shape(part, BF16),) * (count - 1),
        in_specs=[VMEM_SPEC] * 2,
        out_specs=(VMEM_SPEC,) * count,
        compiler_params=PARAMS,
        name="cs",
    )(keep, received)


def pick_columns(ctx, lhs_ref, picked_ref, slots, parity):
    width = lhs_ref.shape[1] // slots
    lanes = max(width, 128)
    for j in range(slots // 2):
        start = jnp.bitwise_xor(ctx, 2 * j + parity) * width
        block = lhs_ref[:, pl.ds(pl.multiple_of(lax.div(start, lanes) * lanes, lanes), lanes)]
        offset = lax.rem(start, lanes)
        chosen = block[:, :width]
        for shift in range(width, lanes, width):
            chosen = jnp.where(offset == shift, block[:, shift : shift + width], chosen)
        picked_ref[:, j * width : (j + 1) * width] = chosen


def grad_kernel(slots, plan, lhs_count, rhs_count, *refs):
    ctx = refs[0][0]
    lhs = refs[1 : 1 + lhs_count]
    rhs = refs[1 + lhs_count : 1 + lhs_count + rhs_count]
    keep_ref, send_ref, picked_ref = refs[1 + lhs_count + rhs_count :]
    for parity, out in ((1, send_ref), (0, keep_ref)):
        column = 0
        for lhs_index, rhs_indices in plan:
            pick_columns(ctx, lhs[lhs_index], picked_ref, slots, parity)
            for index in rhs_indices:
                width = rhs[index].shape[1]
                out[:, column : column + width] = contract_rows(
                    picked_ref[...], rhs[index][...]
                ).astype(BF16)
                column += width


def weight_grads(ctx_index, slots, plan, lhs, rhs):
    width = sum(rhs[i].shape[1] for _, indices in plan for i in indices)
    rows, model = lhs[0].shape
    return pl.pallas_call(
        functools.partial(grad_kernel, slots, plan, len(lhs), len(rhs)),
        out_shape=(shape((model // 2, width), BF16),) * 2,
        in_specs=[SMEM_SPEC] + [VMEM_SPEC] * (len(lhs) + len(rhs)),
        out_specs=(VMEM_SPEC,) * 2,
        scratch_shapes=[pltpu.VMEM((rows, model // 2), BF16)],
        compiler_params=PARAMS,
    )(ctx_index[None], *lhs, *rhs)


def mlp_kernel(shards, *refs):
    n_refs, c_refs = refs[:shards], refs[shards : 2 * shards]
    gate_w, up_w, down_w = refs[2 * shards : 2 * shards + 3]
    outs = refs[2 * shards + 3 :]
    normed_ref, cot_ref, hidden_ref, d_gate_ref, d_up_ref = outs[:5]
    part_refs, acc_ref = outs[5:-1], outs[-1]
    rows = n_refs[0].shape[0]
    for r in range(shards):
        normed_ref[r * rows : (r + 1) * rows, :] = n_refs[r][...]
        cot_ref[r * rows : (r + 1) * rows, :] = c_refs[r][...]
    units = gate_w.shape[1]
    chunk = 256 if units % 256 == 0 else 128
    for start in range(0, units, chunk):
        span = slice(start, start + chunk)
        gate = dot_nn(normed_ref[...], gate_w[:, span])
        up = dot_nn(normed_ref[...], up_w[:, span])
        d_hidden = project_back(cot_ref[...], down_w[span, :])
        sigmoid = 1.0 / (1.0 + jnp.exp(-gate))
        swish = gate * sigmoid
        hidden_ref[:, span] = (swish * up).astype(BF16)
        d_gate = (d_hidden * up * sigmoid * (1.0 + gate * (1.0 - sigmoid))).astype(BF16)
        d_up = (d_hidden * swish).astype(BF16)
        d_gate_ref[:, span] = d_gate
        d_up_ref[:, span] = d_up
        term = project_back(d_gate, gate_w[:, span]) + project_back(d_up, up_w[:, span])
        if start:
            term = term + acc_ref[...]
        if start + chunk < units:
            acc_ref[...] = term
        else:
            for r in range(shards):
                part_refs[r][...] = term[r * rows : (r + 1) * rows].astype(part_refs[r].dtype)


def mlp_side(normed_slots, cot_slots, gate_weight, up_weight, down_weight):
    shards = len(normed_slots)
    rows, model = normed_slots[0].shape
    units = gate_weight.shape[1]
    group_rows = shards * rows
    return pl.pallas_call(
        functools.partial(mlp_kernel, shards),
        out_shape=(shape((group_rows, model), BF16),) * 2
        + (shape((group_rows, units), BF16),) * 3
        + (shape((rows, model), F32),)
        + (shape((rows, model), BF16),) * (shards - 1),
        in_specs=[VMEM_SPEC] * (2 * shards + 3),
        out_specs=(VMEM_SPEC,) * (5 + shards),
        scratch_shapes=[pltpu.VMEM((group_rows, model), F32)],
        compiler_params=PARAMS,
        name="ms",
    )(*normed_slots, *cot_slots, gate_weight, up_weight, down_weight)


def feedforward_kernel(hidden_ref, weight, *part_refs):
    rows = part_refs[0].shape[0]
    for r, out in enumerate(part_refs):
        out[...] = dot_nn(hidden_ref[r * rows : (r + 1) * rows, :], weight[...]).astype(out.dtype)


def feedforward(hidden, down_weight, shards):
    part = (hidden.shape[0] // shards, down_weight.shape[1])
    return pl.pallas_call(
        feedforward_kernel,
        out_shape=(shape(part, F32),) + (shape(part, BF16),) * (shards - 1),
        in_specs=[VMEM_SPEC] * 2,
        out_specs=(VMEM_SPEC,) * shards,
        compiler_params=PARAMS,
        name="fk",
    )(hidden, down_weight)


def start_pieces(pieces, buffers, sems):
    copies = []
    for s in range(len(pieces[0])):
        for which, refs in enumerate(pieces):
            copy = pltpu.make_async_copy(refs[s], buffers[which].at[s], sems.at[which, s])
            copy.start()
            copies.append((s, copy))
    return copies


def wait_pieces(copies, own):
    for s, copy in copies:
        if (s == 0) == own:
            copy.wait()


def causal_mask(info_ref, half, repeat, rows):
    dims = (half, repeat * half)

    def order(axis):
        local = lax.broadcasted_iota(jnp.int32, dims, axis) % half
        shard = jnp.bitwise_xor(local // rows, info_ref[1])
        return shard * rows + local % rows

    return order(0) <= order(1)


def attention_forward_kernel(slots, shards, kv_heads, repeat, *refs):
    info_ref, q_ref, wo_ref = refs[:3]
    refs = refs[3:]
    k_refs, v_refs, refs = refs[:slots], refs[slots : 2 * slots], refs[2 * slots :]
    o_ref, lse_ref, refs = refs[0], refs[1], refs[2:]
    part_refs, refs = refs[:shards], refs[shards:]
    k_buf, v_buf, q_buf, m_a, l_a, acc_a, m_b, l_b, acc_b, sems = refs
    head_dim = acc_a.shape[1]
    half = acc_a.shape[2] // repeat
    rows = 2 * half // shards
    factor = LOG2E / math.sqrt(head_dim)
    copies = start_pieces((k_refs, v_refs), (k_buf, v_buf), sems)
    low = info_ref[0]
    high = 1 - low
    own_block = info_ref[2]
    for p in range(2):
        for kv in range(kv_heads):
            for r in range(repeat):
                column = (kv * repeat + r) * head_dim
                q_buf[p * kv_heads + kv, r * half : (r + 1) * half, :] = q_ref[
                    p * half : (p + 1) * half, column : column + head_dim
                ]

    def load_scores(s, kv, k_half, q_half):
        columns = slice(kv * head_dim, (kv + 1) * head_dim)
        span = pl.ds(pl.multiple_of(k_half * half, half), half)
        scores = project_back(k_buf[s, span, columns], q_buf[q_half * kv_heads + kv])
        return scores, v_buf[s, span, columns]

    def weigh(scores, v, old):
        peak = jnp.max(scores, axis=0, keepdims=True)
        if old is not None:
            peak = jnp.maximum(old[0], peak)
        weights = jnp.exp2((scores - peak) * factor)
        total = jnp.sum(weights, axis=0, keepdims=True)
        mixed = dot_nn(v.T, weights.astype(BF16))
        if old is not None:
            fade = jnp.exp2((old[0] - peak) * factor)
            total = total + old[1] * fade
            mixed = mixed + old[2] * fade
        return peak, total, mixed

    def save(m_ref, l_ref, acc_ref, index, state):
        m_ref[index], l_ref[index], acc_ref[index] = state

    mask = causal_mask(info_ref, half, repeat, rows)
    wait_pieces(copies, True)
    for kv in range(kv_heads):
        for p in (low, high):
            scores, v = load_scores(0, kv, p, p)
            scores = jnp.where(mask, scores, NEGATIVE)
            save(m_b, l_b, acc_b, p * kv_heads + kv, weigh(scores, v, None))
        scores, v = load_scores(0, kv, low, high)
        save(m_a, l_a, acc_a, kv, weigh(scores, v, None))
    wait_pieces(copies, False)

    def step(s, carry):
        chosen = jnp.where(info_ref[2 + s] < own_block, low, high)
        loaded = []
        for kv in range(kv_heads):
            index = chosen * kv_heads + kv
            loaded.append(
                load_scores(s, kv, low, high) + ((m_a[kv], l_a[kv], acc_a[kv]),)
            )
            loaded.append(
                load_scores(s, kv, chosen, chosen) + ((m_b[index], l_b[index], acc_b[index]),)
            )
        states = [weigh(*item) for item in loaded]
        for kv in range(kv_heads):
            save(m_a, l_a, acc_a, kv, states[2 * kv])
            save(m_b, l_b, acc_b, chosen * kv_heads + kv, states[2 * kv + 1])
        return carry

    lax.fori_loop(1, slots, step, 0)

    def finish(p, kv, peak, total, mixed):
        result = mixed / total
        lse_ref[p * kv_heads + kv] = peak * factor + jnp.log(total) * LOG2E
        span = pl.ds(pl.multiple_of(p * half, half), half)
        for r in range(repeat):
            column = (kv * repeat + r) * head_dim
            o_ref[span, column : column + head_dim] = result[
                :, r * half : (r + 1) * half
            ].T.astype(o_ref.dtype)

    for kv in range(kv_heads):
        index = low * kv_heads + kv
        finish(low, kv, m_b[index], l_b[index], acc_b[index])
        index = high * kv_heads + kv
        peak = jnp.maximum(m_a[kv], m_b[index])
        fade_a = jnp.exp2((m_a[kv] - peak) * factor)
        fade_b = jnp.exp2((m_b[index] - peak) * factor)
        finish(
            high,
            kv,
            peak,
            l_a[kv] * fade_a + l_b[index] * fade_b,
            acc_a[kv] * fade_a + acc_b[index] * fade_b,
        )
    part = dot_nn(o_ref[...], wo_ref[...])
    for r in range(shards):
        part_refs[r][...] = part[r * rows : (r + 1) * rows].astype(part_refs[r].dtype)


def attention_forward(info, queries, output_weight, keys, values, head_dim, shards):
    slots = len(keys)
    group_rows, width = queries.shape
    kv_width = keys[0].shape[1]
    kv_heads = kv_width // head_dim
    repeat = width // kv_width
    half = group_rows // 2
    model = output_weight.shape[1]
    wide = repeat * half
    part = (group_rows // shards, model)
    return pl.pallas_call(
        functools.partial(attention_forward_kernel, slots, shards, kv_heads, repeat),
        out_shape=(
            shape((group_rows, width), BF16),
            shape((2 * kv_heads, 1, wide), F32),
            shape(part, F32),
        )
        + (shape(part, BF16),) * (shards - 1),
        in_specs=[SMEM_SPEC, VMEM_SPEC, VMEM_SPEC] + [ANY_SPEC] * (2 * slots),
        out_specs=(VMEM_SPEC,) * (2 + shards),
        scratch_shapes=[
            pltpu.VMEM((slots, group_rows, kv_width), BF16),
            pltpu.VMEM((slots, group_rows, kv_width), BF16),
            pltpu.VMEM((2 * kv_heads, wide, head_dim), BF16),
            pltpu.VMEM((kv_heads, 1, wide), F32),
            pltpu.VMEM((kv_heads, 1, wide), F32),
            pltpu.VMEM((kv_heads, head_dim, wide), F32),
            pltpu.VMEM((2 * kv_heads, 1, wide), F32),
            pltpu.VMEM((2 * kv_heads, 1, wide), F32),
            pltpu.VMEM((2 * kv_heads, head_dim, wide), F32),
            pltpu.SemaphoreType.DMA((2, slots)),
        ],
        compiler_params=PARAMS,
        name="af",
    )(info, queries, output_weight, *keys, *values)


def attention_backward_kernel(slots, shards, kv_heads, repeat, *refs):
    info_ref, q_ref, o_ref, lse_ref, wo_ref = refs[:5]
    refs = refs[5:]
    g_refs, refs = refs[:shards], refs[shards:]
    k_refs, v_refs, refs = refs[:slots], refs[slots : 2 * slots], refs[2 * slots :]
    dq_ref, keep_ref, send_ref, res_ref = refs[:4]
    k_buf, v_buf, q_buf, do_buf, delta_ref, acc_a, acc_b, sems = refs[4:]
    head_dim = acc_a.shape[1]
    half = acc_a.shape[2] // repeat
    rows = 2 * half // shards
    scale = 1.0 / math.sqrt(head_dim)
    factor = LOG2E * scale
    copies = start_pieces((k_refs, v_refs), (k_buf, v_buf), sems)
    low = info_ref[0]
    high = 1 - low
    own_block = info_ref[2]
    for shard in range(shards):
        res_ref[shard * rows : (shard + 1) * rows, :] = g_refs[shard][...]
    d_attended = project_back(res_ref[...], wo_ref[...]).astype(BF16)
    for p in range(2):
        for kv in range(kv_heads):
            for r in range(repeat):
                column = (kv * repeat + r) * head_dim
                do_buf[p * kv_heads + kv, r * half : (r + 1) * half, :] = d_attended[
                    p * half : (p + 1) * half, column : column + head_dim
                ]
    for p in range(2):
        for kv in range(kv_heads):
            index = p * kv_heads + kv
            for r in range(repeat):
                column = (kv * repeat + r) * head_dim
                span = slice(r * half, (r + 1) * half)
                source = (slice(p * half, (p + 1) * half), slice(column, column + head_dim))
                q_buf[index, span, :] = q_ref[source]
                product = do_buf[index, span, :].astype(F32) * o_ref[source].astype(F32)
                delta_ref[index, :, span] = jnp.sum(product.T, axis=0, keepdims=True)

    def load(s, kv, k_half, q_half):
        columns = slice(kv * head_dim, (kv + 1) * head_dim)
        span = pl.ds(pl.multiple_of(k_half * half, half), half)
        index = q_half * kv_heads + kv
        k = k_buf[s, span, columns]
        v = v_buf[s, span, columns]
        q = q_buf[index]
        do = do_buf[index]
        return (
            project_back(k, q), project_back(v, do), k, q, do, lse_ref[index], delta_ref[index]
        )

    def unit(loaded, mask=None):
        scores, d_probs, k, q, do, lse, delta = loaded
        probs = jnp.exp2(scores * factor - lse)
        if mask is not None:
            probs = jnp.where(mask, probs, 0.0)
        d_scores = (probs * (d_probs - delta)).astype(BF16)
        d_value = dot_nn(probs.astype(BF16), do)
        return dot_nn(d_scores, q), d_value, dot_nn(k.T, d_scores)

    group = 2 * half
    kv_width = kv_heads * head_dim

    def store(out_ref, index, p, kv, d_key, d_value):
        column = kv * head_dim
        span = pl.ds(pl.multiple_of(index * group + p * half, half), half)
        out_ref[span, column : column + head_dim] = d_key.astype(BF16)
        out_ref[span, kv_width + column : kv_width + column + head_dim] = d_value.astype(BF16)

    mask = causal_mask(info_ref, half, repeat, rows)
    wait_pieces(copies, True)
    for kv in range(kv_heads):
        dk_high, dv_high, dq = unit(load(0, kv, high, high), mask)
        acc_b[high * kv_heads + kv] = dq
        store(keep_ref, 0, high, kv, dk_high * scale, dv_high)
        dk_low, dv_low, dq = unit(load(0, kv, low, low), mask)
        acc_b[low * kv_heads + kv] = dq
        dk_more, dv_more, dq = unit(load(0, kv, low, high))
        acc_a[kv] = dq
        store(keep_ref, 0, low, kv, (dk_low + dk_more) * scale, dv_low + dv_more)
    wait_pieces(copies, False)

    def step(s, carry):
        earlier = info_ref[2 + s] < own_block
        chosen = jnp.where(earlier, low, high)
        keep = jnp.where(earlier, 1.0, 0.0)
        loaded = []
        for kv in range(kv_heads):
            loaded.append(load(s, kv, low, high))
            loaded.append(load(s, kv, chosen, chosen))
        units = [unit(item) for item in loaded]
        for kv in range(kv_heads):
            index = chosen * kv_heads + kv
            dq_a, dq_b = units[2 * kv][2], units[2 * kv + 1][2]
            acc_a[kv] = acc_a[kv] + dq_a
            acc_b[index] = acc_b[index] + dq_b

        def write(out_ref):
            index = lax.div(s, 2)
            for kv in range(kv_heads):
                dk_low, dv_low, _ = units[2 * kv]
                dk_sel, dv_sel, _ = units[2 * kv + 1]
                rest = 1.0 - keep
                store(
                    out_ref, index, low, kv, (dk_low + dk_sel * keep) * scale, dv_low + dv_sel * keep
                )
                store(out_ref, index, high, kv, dk_sel * (rest * scale), dv_sel * rest)

        odd = lax.rem(s, 2) == 1
        pl.when(odd)(lambda: write(send_ref))
        pl.when(jnp.logical_not(odd))(lambda: write(keep_ref))
        return carry

    lax.fori_loop(1, slots, step, 0)

    def finish(p, kv, values):
        span = pl.ds(pl.multiple_of(p * half, half), half)
        for r in range(repeat):
            column = (kv * repeat + r) * head_dim
            dq_ref[span, column : column + head_dim] = (
                values[:, r * half : (r + 1) * half].T * scale
            )

    for kv in range(kv_heads):
        finish(low, kv, acc_b[low * kv_heads + kv])
        finish(high, kv, acc_b[high * kv_heads + kv] + acc_a[kv])


def attention_backward(
    info, queries, attended, lse, output_weight, d_residual_slots, keys, values, head_dim
):
    slots = len(keys)
    shards = len(d_residual_slots)
    group_rows, width = queries.shape
    kv_width = keys[0].shape[1]
    kv_heads = kv_width // head_dim
    repeat = width // kv_width
    half = group_rows // 2
    wide = repeat * half
    piece = shape((slots // 2 * group_rows, 2 * kv_width), BF16)
    model = output_weight.shape[1]
    return pl.pallas_call(
        functools.partial(attention_backward_kernel, slots, shards, kv_heads, repeat),
        out_shape=(
            shape((group_rows, width), F32), piece, piece, shape((group_rows, model), BF16)
        ),
        in_specs=[SMEM_SPEC] + [VMEM_SPEC] * (4 + shards) + [ANY_SPEC] * (2 * slots),
        out_specs=(VMEM_SPEC,) * 4,
        scratch_shapes=[
            pltpu.VMEM((slots, group_rows, kv_width), BF16),
            pltpu.VMEM((slots, group_rows, kv_width), BF16),
            pltpu.VMEM((2 * kv_heads, wide, head_dim), BF16),
            pltpu.VMEM((2 * kv_heads, wide, head_dim), BF16),
            pltpu.VMEM((2 * kv_heads, 1, wide), F32),
            pltpu.VMEM((kv_heads, head_dim, wide), F32),
            pltpu.VMEM((2 * kv_heads, head_dim, wide), F32),
            pltpu.SemaphoreType.DMA((2, slots)),
        ],
        compiler_params=PARAMS,
        name="ab",
    )(
        info, queries, attended, lse, output_weight, *d_residual_slots, *keys, *values
    )


def body(
    layer_input,
    out_cotangent,
    block_map,
    first_gain,
    query_weight,
    key_weight,
    value_weight,
    query_gain,
    key_gain,
    output_weight,
    second_gain,
    gate_weight,
    up_weight,
    down_weight,
):
    groups = lax.axis_size("ctx")
    shards = lax.axis_size("tp")
    ctx_index = lax.axis_index("ctx")
    tp_index = lax.axis_index("tp")
    bits = list(range(1, groups.bit_length() - 1))
    head_dim = query_gain.shape[0]
    rows = layer_input.shape[0]
    group_rows = rows * shards
    half = group_rows // 2

    local = jnp.arange(group_rows, dtype=jnp.int32)
    within = jnp.bitwise_xor(local // rows, tp_index) * rows + local % rows
    own_block = lax.dynamic_index_in_dim(block_map, ctx_index, keepdims=False)
    block = jnp.where(within < half, own_block, 2 * groups - 1 - own_block)
    positions = block * half + within % half
    slot_blocks = jnp.take(block_map, jnp.bitwise_xor(jnp.arange(groups), ctx_index), axis=0)
    info = jnp.concatenate(
        [
            jnp.stack([tp_index // (shards // 2), tp_index % (shards // 2)]).astype(jnp.int32),
            slot_blocks.astype(jnp.int32),
        ]
    )

    x_slots = gather_slots(layer_input, "tp")
    cosine, sine = rope_tables(positions, head_dim)
    normed_a, key_linear, key_rows, value_rows = key_value(
        x_slots, first_gain, key_weight, value_weight, key_gain, cosine, sine
    )
    keys, values = gather_ctx(key_rows, value_rows, bits)
    cotangent_slots = gather_slots(after(out_cotangent, *x_slots), "tp")
    query_linear, queries = query_side(normed_a, query_weight, query_gain, cosine, sine)
    attended, lse, *attention_parts = attention_forward(
        info, queries, output_weight, keys, values, head_dim, shards
    )
    inputs_float = layer_input.astype(F32)
    residual = inputs_float + scatter_slots(attention_parts, "tp")
    normed_second, second_pull = jax.vjp(rms_apply, residual, second_gain)
    normed_slots = gather_slots(normed_second.astype(BF16), "tp")
    normed_b, cotangent_all, hidden, d_gate, d_upward, *second_parts = mlp_side(
        normed_slots, cotangent_slots, gate_weight, up_weight, down_weight
    )
    mlp_keep, mlp_send = weight_grads(
        ctx_index,
        groups,
        ((0, (0, 1)), (1, (2,))),
        (normed_b, cotangent_all),
        (d_gate, d_upward, hidden),
    )
    feedforward_parts = feedforward(hidden, down_weight, shards)
    d_second = scatter_slots(second_parts, "tp")
    mlp_own, mlp_got = exchange_ctx(mlp_keep, mlp_send)
    d_residual_norm, second_gain_part = second_pull(d_second)
    d_residual = out_cotangent.astype(F32) + d_residual_norm
    d_residual_slots = gather_slots(d_residual.astype(BF16), "tp")
    dq, dkv_keep, dkv_send, d_residual_all = attention_backward(
        info, queries, attended, lse, output_weight, d_residual_slots, keys, values, head_dim
    )
    dkv_own, dkv_got = exchange_ctx(dkv_keep, dkv_send)
    d_query_b, query_term, query_gain_part = query_backward(
        dq, query_linear, query_weight, query_gain, cosine, sine
    )
    feedforward_parts = after(tuple(feedforward_parts), dq)
    feedforward_part = scatter_slots(feedforward_parts, "tp")
    units = d_gate.shape[1]
    mlp_total = total_of(mlp_own, mlp_got)
    gate_sum, upward_sum = mlp_total[:, :units], mlp_total[:, units : 2 * units]
    down_sum = mlp_total[:, 2 * units :].T
    dkv_got, (gate_sum, upward_sum, down_sum) = hold(dkv_got, gate_sum, upward_sum, down_sum)
    query_keep, query_send = weight_grads(
        ctx_index, groups, ((0, (0,)), (1, (1,))), (d_residual_all, normed_a), (attended, d_query_b)
    )
    d_key_b, d_value_b, key_gain_part, first_gain_part, *first_parts = first_side(
        dkv_own,
        dkv_got,
        key_linear,
        key_weight,
        value_weight,
        key_gain,
        cosine,
        sine,
        query_term,
        normed_a,
        shards,
    )
    d_first = scatter_slots(first_parts, "tp")
    key_keep, key_send = weight_grads(
        ctx_index, groups, ((0, (0, 1)),), (normed_a,), (d_key_b, d_value_b)
    )
    gains = jnp.concatenate(
        [first_gain_part[0] / first_gain, second_gain_part, query_gain_part[0], key_gain_part[0]]
    )
    query_own, query_got = exchange_ctx(query_keep, query_send)
    key_own, key_got = exchange_ctx(key_keep, key_send)
    gains = sum_all(gains)
    first_pull = jax.vjp(lambda v: rms_apply(v, first_gain), inputs_float)[1]
    input_grad = d_residual + first_pull(d_first)[0]

    layer_output = residual + feedforward_part
    query_total = total_of(query_own, query_got)
    key_total = total_of(key_own, key_got)
    query_width, key_width = attended.shape[1], d_key_b.shape[1]
    output_sum, query_sum = query_total[:, :query_width], query_total[:, query_width:]
    key_sum, value_sum = key_total[:, :key_width], key_total[:, key_width:]
    width = first_gain.shape[0]
    return (
        layer_output,
        input_grad,
        gains[:width],
        query_sum,
        key_sum,
        value_sum,
        gains[2 * width : 2 * width + head_dim],
        gains[2 * width + head_dim :],
        output_sum.T,
        gains[width : 2 * width],
        gate_sum,
        upward_sum,
        down_sum,
    )


def solution(mesh):
    return jax.shard_map(
        body,
        mesh=mesh,
        in_specs=(
            P(("ctx", "tp"), None),
            P(("ctx", "tp"), None),
            P(),
            P(),
            P(None, "tp"),
            P(None, "tp"),
            P(None, "tp"),
            P(),
            P(),
            P("tp", None),
            P(),
            P(None, "tp"),
            P(None, "tp"),
            P("tp", None),
        ),
        out_specs=(
            P(("ctx", "tp"), None),
            P(("ctx", "tp"), None),
            P(),
            P("ctx", "tp"),
            P("ctx", "tp"),
            P("ctx", "tp"),
            P(),
            P(),
            P("tp", "ctx"),
            P(),
            P("ctx", "tp"),
            P("ctx", "tp"),
            P("tp", "ctx"),
        ),
        check_vma=False,
    )
```

```python
import functools
import math

import jax
import jax.numpy as jnp
from jax import lax
from jax.experimental import pallas as pl
from jax.experimental.pallas import tpu as pltpu
from jax.sharding import PartitionSpec as P


EPSILON = 1e-06
ROPE_BASE = 1000000.0
NEGATIVE = -1e30
F32 = jnp.float32
BF16 = jnp.bfloat16
VMEM_LIMIT = 56 * 1024 * 1024


def rms_apply(values, scaling):
    factor = lax.rsqrt(jnp.mean(values * values, axis=-1, keepdims=True) + EPSILON)
    return values * factor * scaling


def rope_tables(positions, head_dim):
    half_dim = head_dim // 2
    inverse = jnp.exp(
        jnp.arange(half_dim).astype(F32) * (-2.0 * math.log(ROPE_BASE) / head_dim)
    )
    angles = positions.astype(F32)[:, None] * inverse[None, :]
    cosine, sine = jnp.cos(angles), jnp.sin(angles)
    cosine_table = jnp.concatenate([cosine, cosine], axis=-1)
    signed_sine_table = jnp.concatenate([-sine, sine], axis=-1)
    return (cosine_table, signed_sine_table)


def contract_rows(left, right):
    return lax.dot_general(left, right, (((0,), (0,)), ((), ())), preferred_element_type=F32)


def project_back(left, right):
    return lax.dot_general(left, right, (((1,), (1,)), ((), ())), preferred_element_type=F32)


def dot_nn(left, right):
    return lax.dot_general(left, right, (((1,), (0,)), ((), ())), preferred_element_type=F32)


def swap(values, axis, mask):
    size = lax.axis_size(axis)
    return lax.ppermute(values, axis, [(k, k ^ mask) for k in range(size)])


def after(values, *others):
    return lax.optimization_barrier((values,) + others)[0]


def gather_slots(values, axis):
    have = {0: values}
    for bit in reversed(range(lax.axis_size(axis).bit_length() - 1)):
        mask = 1 << bit
        for m in sorted(have):
            have[m ^ mask] = swap(have[m], axis, mask)
    return [have[m] for m in sorted(have)]


def scatter_slots(parts, axis):
    sums = {m: part for m, part in enumerate(parts)}
    for hop, bit in enumerate(range(lax.axis_size(axis).bit_length() - 1)):
        mask = 1 << bit
        for m in sorted((m for m in sums if m & mask), reverse=True):
            going = sums.pop(m).astype(BF16)
            last = (m ^ mask) == 0
            if last and hop == 0:
                rest = {k: v for k, v in sums.items() if k}
                going, rest = lax.optimization_barrier((going, rest))
                sums.update(rest)
            got = swap(going, axis, mask)
            sums[m ^ mask] = sums[m ^ mask].astype(F32) + got.astype(F32)
    return sums[0]


def hold(values, *others):
    return lax.optimization_barrier((values, others))


def gather_ctx(keys, values, bits):
    streams = [{0: keys}, {0: values}]
    for stage in range(len(bits) + 1):
        for have, order in zip(streams, (bits + [0], bits[::-1] + [0])):
            mask = 1 << order[stage]
            have.update({m ^ mask: swap(v, "ctx", mask) for m, v in have.items()})
    return [[have[m] for m in sorted(have)] for have in streams]


def exchange_ctx(keep, send):
    received = swap(send, "ctx", 1)
    own, *going = core_sum(keep, received, lax.axis_size("ctx") // 2)
    return own, [swap(part, "ctx", 2 * (j + 1)) for j, part in enumerate(going)]


def total_of(own, pieces):
    return sum([piece.astype(F32) for piece in pieces], own)


def sum_ctx(values):
    values = values + swap(values, "ctx", 1)
    masks = range(2, lax.axis_size("ctx"), 2)
    return sum([swap(values, "ctx", m) for m in masks], values)


VMEM_SPEC = pl.BlockSpec(memory_space=pltpu.VMEM)
ANY_SPEC = pl.BlockSpec(memory_space=pl.ANY)
SMEM_SPEC = pl.BlockSpec(memory_space=pltpu.SMEM)
PARAMS = pltpu.CompilerParams(vmem_limit_bytes=VMEM_LIMIT)
GAIN_ROWS = 16
LOG2E = math.log2(math.e)


def shape(dims, dtype):
    return jax.ShapeDtypeStruct(tuple(dims), dtype)


def rotate_lanes(values):
    return pltpu.roll(values, values.shape[-1] // 2, axis=values.ndim - 1)


def head_forward(linear, gain, cosine, sine):
    factor = lax.rsqrt(jnp.mean(linear * linear, axis=-1, keepdims=True) + EPSILON)
    normed = linear * factor * gain
    return normed * cosine + rotate_lanes(normed) * sine


def key_value_kernel(size, *refs):
    x_refs = refs[:size]
    gain, key_w, value_w, key_gain, cosine, sine = refs[size : size + 6]
    normed_ref, linear_ref, key_ref, value_ref = refs[size + 6 :]
    rows = x_refs[0].shape[0]
    head_dim = key_gain.shape[1]
    for r in range(size):
        span = slice(r * rows, (r + 1) * rows)
        x = x_refs[r][...].astype(F32)
        factor = lax.rsqrt(jnp.mean(x * x, axis=-1, keepdims=True) + EPSILON)
        normed = (x * factor * gain[...]).astype(BF16)
        normed_ref[span, :] = normed
        linear = dot_nn(normed, key_w[...])
        linear_ref[span, :] = linear
        for h in range(linear.shape[1] // head_dim):
            columns = slice(h * head_dim, (h + 1) * head_dim)
            key_ref[span, columns] = head_forward(
                linear[:, columns], key_gain[...], cosine[span, :], sine[span, :]
            ).astype(BF16)
        value_ref[span, :] = dot_nn(normed, value_w[...]).astype(BF16)


def key_value(x_slots, gain, key_weight, value_weight, key_gain, cosine, sine):
    size = len(x_slots)
    group_rows = size * x_slots[0].shape[0]
    width = key_weight.shape[1]
    return pl.pallas_call(
        functools.partial(key_value_kernel, size),
        out_shape=(
            shape((group_rows, x_slots[0].shape[1]), BF16),
            shape((group_rows, width), F32),
            shape((group_rows, width), BF16),
            shape((group_rows, width), BF16),
        ),
        in_specs=[VMEM_SPEC] * (size + 6),
        out_specs=(VMEM_SPEC,) * 4,
        compiler_params=PARAMS,
        name="kv",
    )(*x_slots, gain[None], key_weight, value_weight, key_gain[None], cosine, sine)


def query_kernel(normed_ref, weight_ref, gain, cosine, sine, linear_ref, query_ref):
    head_dim = gain.shape[1]
    chunk = min(256, normed_ref.shape[0])
    for start in range(0, normed_ref.shape[0], chunk):
        span = slice(start, start + chunk)
        linear = dot_nn(normed_ref[span, :], weight_ref[...])
        linear_ref[span, :] = linear
        for h in range(linear.shape[1] // head_dim):
            columns = slice(h * head_dim, (h + 1) * head_dim)
            query_ref[span, columns] = head_forward(
                linear[:, columns], gain[...], cosine[span, :], sine[span, :]
            ).astype(BF16)


def query_side(normed, weight, gain, cosine, sine):
    dims = (normed.shape[0], weight.shape[1])
    return pl.pallas_call(
        query_kernel,
        out_shape=(shape(dims, F32), shape(dims, BF16)),
        in_specs=[VMEM_SPEC] * 5,
        out_specs=(VMEM_SPEC,) * 2,
        compiler_params=PARAMS,
        name="qs",
    )(normed, weight, gain[None], cosine, sine)


def head_backward(d, linear, gain, cosine, sine):
    d = d * cosine - rotate_lanes(d) * sine
    factor = lax.rsqrt(jnp.mean(linear * linear, axis=-1, keepdims=True) + EPSILON)
    unit = linear * factor
    gain_part = jnp.sum(d * unit, axis=0, keepdims=True)
    d = d * gain
    inner = jnp.mean(d * unit, axis=-1, keepdims=True)
    return (d - unit * inner) * factor, gain_part


def query_backward_kernel(d_ref, linear_ref, weight, gain, cosine, sine, out_ref, term_ref, gain_ref):
    head_dim = gain.shape[1]
    chunk = min(256, d_ref.shape[0])
    total = jnp.zeros((1, head_dim), F32)
    for start in range(0, d_ref.shape[0], chunk):
        span = slice(start, start + chunk)
        for h in range(d_ref.shape[1] // head_dim):
            columns = slice(h * head_dim, (h + 1) * head_dim)
            d, part = head_backward(
                d_ref[span, columns],
                linear_ref[span, columns],
                gain[...],
                cosine[span, :],
                sine[span, :],
            )
            total = total + part
            out_ref[span, columns] = d.astype(BF16)
        term_ref[span, :] = project_back(out_ref[span, :], weight[...])
    gain_ref[...] = total


def query_backward(d, linear, weight, gain, cosine, sine):
    return pl.pallas_call(
        query_backward_kernel,
        out_shape=(
            shape(d.shape, BF16),
            shape((d.shape[0], weight.shape[0]), F32),
            shape((1, gain.shape[0]), F32),
        ),
        in_specs=[VMEM_SPEC] * 6,
        out_specs=(VMEM_SPEC,) * 3,
        compiler_params=PARAMS,
        name="qb",
    )(d, linear, weight, gain[None], cosine, sine)


def first_kernel(pieces, shards, *refs):
    own_ref, got = refs[0], refs[1 : 1 + pieces]
    linear_ref, key_w, value_w, gain, cosine, sine, term_ref, normed_ref = refs[
        1 + pieces : 9 + pieces
    ]
    second_ref, query_gain_ref, dk_ref, dv_ref, *part_refs = refs[9 + pieces :]
    head_dim = gain.shape[1]
    width = linear_ref.shape[1]
    rows = own_ref.shape[0] // shards
    total = jnp.zeros((1, head_dim), F32)
    both = own_ref[...]
    for ref in got:
        both = both + ref[...].astype(F32)
    for h in range(width // head_dim):
        columns = slice(h * head_dim, (h + 1) * head_dim)
        d, part = head_backward(
            both[:, columns], linear_ref[:, columns], gain[...], cosine[...], sine[...]
        )
        total = total + part
        dk_ref[:, columns] = d.astype(BF16)
    dv_ref[...] = both[:, width:].astype(BF16)
    term = term_ref[...] + project_back(dk_ref[...], key_w[...])
    term = term + project_back(dv_ref[...], value_w[...])
    model = normed_ref.shape[1]
    first = jnp.sum(term * normed_ref[...].astype(F32), axis=0, keepdims=True)
    heads = jnp.concatenate(
        [query_gain_ref[...], total, jnp.zeros((1, model - 2 * head_dim), F32)], axis=1
    )
    row = lax.broadcasted_iota(jnp.int32, (GAIN_ROWS, model), 0)
    gains = jnp.where(row == 0, first, jnp.where(row == 1, second_ref[...], heads))
    gains = jnp.where(row < 3, gains, 0.0)
    for r in range(shards):
        part_refs[r][:rows, :] = term[r * rows : (r + 1) * rows].astype(part_refs[r].dtype)
        part_refs[r][rows:, :] = gains.astype(part_refs[r].dtype)


def first_side(own, got, linear, key_weight, value_weight, gain, cosine, sine, *rest):
    term, normed, second_gain_part, query_gain_part, shards = rest
    model = normed.shape[1]
    part = (term.shape[0] // shards + GAIN_ROWS, model)
    return pl.pallas_call(
        functools.partial(first_kernel, len(got), shards),
        out_shape=(shape(linear.shape, BF16), shape(linear.shape, BF16), shape(part, F32))
        + (shape(part, BF16),) * (shards - 1),
        in_specs=[VMEM_SPEC] * (11 + len(got)),
        out_specs=(VMEM_SPEC,) * (2 + shards),
        compiler_params=PARAMS,
        name="fs",
    )(
        own,
        *got,
        linear,
        key_weight,
        value_weight,
        gain[None],
        cosine,
        sine,
        term,
        normed,
        second_gain_part[None],
        query_gain_part,
    )


def core_sum_kernel(keep_ref, got_ref, *outs):
    rows = outs[0].shape[0]
    for j, out in enumerate(outs):
        span = slice(j * rows, (j + 1) * rows)
        out[...] = (keep_ref[span, :].astype(F32) + got_ref[span, :].astype(F32)).astype(out.dtype)


def core_sum(keep, received, count):
    part = (keep.shape[0] // count, keep.shape[1])
    return pl.pallas_call(
        core_sum_kernel,
        out_shape=(shape(part, F32),) + (shape(part, BF16),) * (count - 1),
        in_specs=[VMEM_SPEC] * 2,
        out_specs=(VMEM_SPEC,) * count,
        compiler_params=PARAMS,
        name="cs",
    )(keep, received)


def pick_columns(ctx, lhs_ref, picked_ref, slots, parity):
    width = lhs_ref.shape[1] // slots
    lanes = max(width, 128)
    for j in range(slots // 2):
        start = jnp.bitwise_xor(ctx, 2 * j + parity) * width
        block = lhs_ref[:, pl.ds(pl.multiple_of(lax.div(start, lanes) * lanes, lanes), lanes)]
        offset = lax.rem(start, lanes)
        chosen = block[:, :width]
        for shift in range(width, lanes, width):
            chosen = jnp.where(offset == shift, block[:, shift : shift + width], chosen)
        picked_ref[:, j * width : (j + 1) * width] = chosen


def grad_kernel(slots, plan, lhs_count, rhs_count, *refs):
    ctx = refs[0][0]
    lhs = refs[1 : 1 + lhs_count]
    rhs = refs[1 + lhs_count : 1 + lhs_count + rhs_count]
    keep_ref, send_ref, picked_ref = refs[1 + lhs_count + rhs_count :]
    for parity, out in ((1, send_ref), (0, keep_ref)):
        column = 0
        for lhs_index, rhs_indices in plan:
            pick_columns(ctx, lhs[lhs_index], picked_ref, slots, parity)
            for index in rhs_indices:
                width = rhs[index].shape[1]
                out[:, column : column + width] = contract_rows(
                    picked_ref[...], rhs[index][...]
                ).astype(BF16)
                column += width


def weight_grads(ctx_index, slots, plan, lhs, rhs):
    width = sum(rhs[i].shape[1] for _, indices in plan for i in indices)
    rows, model = lhs[0].shape
    return pl.pallas_call(
        functools.partial(grad_kernel, slots, plan, len(lhs), len(rhs)),
        out_shape=(shape((model // 2, width), BF16),) * 2,
        in_specs=[SMEM_SPEC] + [VMEM_SPEC] * (len(lhs) + len(rhs)),
        out_specs=(VMEM_SPEC,) * 2,
        scratch_shapes=[pltpu.VMEM((rows, model // 2), BF16)],
        compiler_params=PARAMS,
    )(ctx_index[None], *lhs, *rhs)


def mlp_kernel(shards, *refs):
    n_refs, c_refs = refs[:shards], refs[shards : 2 * shards]
    gate_w, up_w, down_w = refs[2 * shards : 2 * shards + 3]
    outs = refs[2 * shards + 3 :]
    normed_ref, cot_ref, hidden_ref, d_gate_ref, d_up_ref = outs[:5]
    part_refs, acc_ref = outs[5:-1], outs[-1]
    rows = n_refs[0].shape[0]
    for r in range(shards):
        normed_ref[r * rows : (r + 1) * rows, :] = n_refs[r][...]
        cot_ref[r * rows : (r + 1) * rows, :] = c_refs[r][...]
    units = gate_w.shape[1]
    chunk = 256 if units % 256 == 0 else 128
    for start in range(0, units, chunk):
        span = slice(start, start + chunk)
        gate = dot_nn(normed_ref[...], gate_w[:, span])
        up = dot_nn(normed_ref[...], up_w[:, span])
        d_hidden = project_back(cot_ref[...], down_w[span, :])
        sigmoid = 1.0 / (1.0 + jnp.exp(-gate))
        swish = gate * sigmoid
        hidden_ref[:, span] = (swish * up).astype(BF16)
        d_gate = (d_hidden * up * sigmoid * (1.0 + gate * (1.0 - sigmoid))).astype(BF16)
        d_up = (d_hidden * swish).astype(BF16)
        d_gate_ref[:, span] = d_gate
        d_up_ref[:, span] = d_up
        term = project_back(d_gate, gate_w[:, span]) + project_back(d_up, up_w[:, span])
        if start:
            term = term + acc_ref[...]
        if start + chunk < units:
            acc_ref[...] = term
        else:
            for r in range(shards):
                part_refs[r][...] = term[r * rows : (r + 1) * rows].astype(part_refs[r].dtype)


def mlp_side(normed_slots, cot_slots, gate_weight, up_weight, down_weight):
    shards = len(normed_slots)
    rows, model = normed_slots[0].shape
    units = gate_weight.shape[1]
    group_rows = shards * rows
    return pl.pallas_call(
        functools.partial(mlp_kernel, shards),
        out_shape=(shape((group_rows, model), BF16),) * 2
        + (shape((group_rows, units), BF16),) * 3
        + (shape((rows, model), F32),)
        + (shape((rows, model), BF16),) * (shards - 1),
        in_specs=[VMEM_SPEC] * (2 * shards + 3),
        out_specs=(VMEM_SPEC,) * (5 + shards),
        scratch_shapes=[pltpu.VMEM((group_rows, model), F32)],
        compiler_params=PARAMS,
        name="ms",
    )(*normed_slots, *cot_slots, gate_weight, up_weight, down_weight)


def feedforward_kernel(hidden_ref, weight, *part_refs):
    rows = part_refs[0].shape[0]
    for r, out in enumerate(part_refs):
        out[...] = dot_nn(hidden_ref[r * rows : (r + 1) * rows, :], weight[...]).astype(out.dtype)


def feedforward(hidden, down_weight, shards):
    part = (hidden.shape[0] // shards, down_weight.shape[1])
    return pl.pallas_call(
        feedforward_kernel,
        out_shape=(shape(part, F32),) + (shape(part, BF16),) * (shards - 1),
        in_specs=[VMEM_SPEC] * 2,
        out_specs=(VMEM_SPEC,) * shards,
        compiler_params=PARAMS,
        name="fk",
    )(hidden, down_weight)


def start_pieces(pieces, buffers, sems):
    copies = []
    for s in range(len(pieces[0])):
        for which, refs in enumerate(pieces):
            copy = pltpu.make_async_copy(refs[s], buffers[which].at[s], sems.at[which, s])
            copy.start()
            copies.append((s, copy))
    return copies


def wait_pieces(copies, own):
    for s, copy in copies:
        if (s == 0) == own:
            copy.wait()


def causal_mask(info_ref, half, repeat, rows):
    dims = (half, repeat * half)

    def order(axis):
        local = lax.broadcasted_iota(jnp.int32, dims, axis) % half
        shard = jnp.bitwise_xor(local // rows, info_ref[1])
        return shard * rows + local % rows

    return order(0) <= order(1)


def attention_forward_kernel(slots, shards, kv_heads, repeat, *refs):
    info_ref, q_ref, wo_ref = refs[:3]
    refs = refs[3:]
    k_refs, v_refs, refs = refs[:slots], refs[slots : 2 * slots], refs[2 * slots :]
    o_ref, lse_ref, refs = refs[0], refs[1], refs[2:]
    part_refs, refs = refs[:shards], refs[shards:]
    k_buf, v_buf, q_buf, m_a, l_a, acc_a, m_b, l_b, acc_b, sems = refs
    head_dim = acc_a.shape[1]
    half = acc_a.shape[2] // repeat
    rows = 2 * half // shards
    factor = LOG2E / math.sqrt(head_dim)
    copies = start_pieces((k_refs, v_refs), (k_buf, v_buf), sems)
    low = info_ref[0]
    high = 1 - low
    own_block = info_ref[2]
    for p in range(2):
        for kv in range(kv_heads):
            for r in range(repeat):
                column = (kv * repeat + r) * head_dim
                q_buf[p * kv_heads + kv, r * half : (r + 1) * half, :] = q_ref[
                    p * half : (p + 1) * half, column : column + head_dim
                ]

    def load_scores(s, kv, k_half, q_half):
        columns = slice(kv * head_dim, (kv + 1) * head_dim)
        span = pl.ds(pl.multiple_of(k_half * half, half), half)
        scores = project_back(k_buf[s, span, columns], q_buf[q_half * kv_heads + kv])
        return scores, v_buf[s, span, columns]

    def weigh(scores, v, old):
        peak = jnp.max(scores, axis=0, keepdims=True)
        if old is not None:
            peak = jnp.maximum(old[0], peak)
        weights = jnp.exp2((scores - peak) * factor)
        total = jnp.sum(weights, axis=0, keepdims=True)
        mixed = dot_nn(v.T, weights.astype(BF16))
        if old is not None:
            fade = jnp.exp2((old[0] - peak) * factor)
            total = total + old[1] * fade
            mixed = mixed + old[2] * fade
        return peak, total, mixed

    def save(m_ref, l_ref, acc_ref, index, state):
        m_ref[index], l_ref[index], acc_ref[index] = state

    mask = causal_mask(info_ref, half, repeat, rows)
    wait_pieces(copies, True)
    for kv in range(kv_heads):
        for p in (low, high):
            scores, v = load_scores(0, kv, p, p)
            scores = jnp.where(mask, scores, NEGATIVE)
            save(m_b, l_b, acc_b, p * kv_heads + kv, weigh(scores, v, None))
        scores, v = load_scores(0, kv, low, high)
        save(m_a, l_a, acc_a, kv, weigh(scores, v, None))
    wait_pieces(copies, False)

    def step(s, carry):
        chosen = jnp.where(info_ref[2 + s] < own_block, low, high)
        loaded = []
        for kv in range(kv_heads):
            index = chosen * kv_heads + kv
            loaded.append(
                load_scores(s, kv, low, high) + ((m_a[kv], l_a[kv], acc_a[kv]),)
            )
            loaded.append(
                load_scores(s, kv, chosen, chosen) + ((m_b[index], l_b[index], acc_b[index]),)
            )
        states = [weigh(*item) for item in loaded]
        for kv in range(kv_heads):
            save(m_a, l_a, acc_a, kv, states[2 * kv])
            save(m_b, l_b, acc_b, chosen * kv_heads + kv, states[2 * kv + 1])
        return carry

    lax.fori_loop(1, slots, step, 0)

    def finish(p, kv, peak, total, mixed):
        result = mixed / total
        lse_ref[p * kv_heads + kv] = peak * factor + jnp.log(total) * LOG2E
        span = pl.ds(pl.multiple_of(p * half, half), half)
        for r in range(repeat):
            column = (kv * repeat + r) * head_dim
            o_ref[span, column : column + head_dim] = result[
                :, r * half : (r + 1) * half
            ].T.astype(o_ref.dtype)

    for kv in range(kv_heads):
        index = low * kv_heads + kv
        finish(low, kv, m_b[index], l_b[index], acc_b[index])
        index = high * kv_heads + kv
        peak = jnp.maximum(m_a[kv], m_b[index])
        fade_a = jnp.exp2((m_a[kv] - peak) * factor)
        fade_b = jnp.exp2((m_b[index] - peak) * factor)
        finish(
            high,
            kv,
            peak,
            l_a[kv] * fade_a + l_b[index] * fade_b,
            acc_a[kv] * fade_a + acc_b[index] * fade_b,
        )
    part = dot_nn(o_ref[...], wo_ref[...])
    for r in range(shards):
        part_refs[r][...] = part[r * rows : (r + 1) * rows].astype(part_refs[r].dtype)


def attention_forward(info, queries, output_weight, keys, values, head_dim, shards):
    slots = len(keys)
    group_rows, width = queries.shape
    kv_width = keys[0].shape[1]
    kv_heads = kv_width // head_dim
    repeat = width // kv_width
    half = group_rows // 2
    model = output_weight.shape[1]
    wide = repeat * half
    part = (group_rows // shards, model)
    return pl.pallas_call(
        functools.partial(attention_forward_kernel, slots, shards, kv_heads, repeat),
        out_shape=(
            shape((group_rows, width), BF16),
            shape((2 * kv_heads, 1, wide), F32),
            shape(part, F32),
        )
        + (shape(part, BF16),) * (shards - 1),
        in_specs=[SMEM_SPEC, VMEM_SPEC, VMEM_SPEC] + [ANY_SPEC] * (2 * slots),
        out_specs=(VMEM_SPEC,) * (2 + shards),
        scratch_shapes=[
            pltpu.VMEM((slots, group_rows, kv_width), BF16),
            pltpu.VMEM((slots, group_rows, kv_width), BF16),
            pltpu.VMEM((2 * kv_heads, wide, head_dim), BF16),
            pltpu.VMEM((kv_heads, 1, wide), F32),
            pltpu.VMEM((kv_heads, 1, wide), F32),
            pltpu.VMEM((kv_heads, head_dim, wide), F32),
            pltpu.VMEM((2 * kv_heads, 1, wide), F32),
            pltpu.VMEM((2 * kv_heads, 1, wide), F32),
            pltpu.VMEM((2 * kv_heads, head_dim, wide), F32),
            pltpu.SemaphoreType.DMA((2, slots)),
        ],
        compiler_params=PARAMS,
        name="af",
    )(info, queries, output_weight, *keys, *values)


def attention_backward_kernel(slots, shards, kv_heads, repeat, *refs):
    info_ref, q_ref, o_ref, lse_ref, wo_ref = refs[:5]
    refs = refs[5:]
    g_refs, refs = refs[:shards], refs[shards:]
    k_refs, v_refs, refs = refs[:slots], refs[slots : 2 * slots], refs[2 * slots :]
    dq_ref, keep_ref, send_ref, res_ref = refs[:4]
    k_buf, v_buf, q_buf, do_buf, delta_ref, acc_a, acc_b, sems = refs[4:]
    head_dim = acc_a.shape[1]
    half = acc_a.shape[2] // repeat
    rows = 2 * half // shards
    scale = 1.0 / math.sqrt(head_dim)
    factor = LOG2E * scale
    copies = start_pieces((k_refs, v_refs), (k_buf, v_buf), sems)
    low = info_ref[0]
    high = 1 - low
    own_block = info_ref[2]
    for shard in range(shards):
        res_ref[shard * rows : (shard + 1) * rows, :] = g_refs[shard][...]
    d_attended = project_back(res_ref[...], wo_ref[...]).astype(BF16)
    for p in range(2):
        for kv in range(kv_heads):
            for r in range(repeat):
                column = (kv * repeat + r) * head_dim
                do_buf[p * kv_heads + kv, r * half : (r + 1) * half, :] = d_attended[
                    p * half : (p + 1) * half, column : column + head_dim
                ]
    for p in range(2):
        for kv in range(kv_heads):
            index = p * kv_heads + kv
            for r in range(repeat):
                column = (kv * repeat + r) * head_dim
                span = slice(r * half, (r + 1) * half)
                source = (slice(p * half, (p + 1) * half), slice(column, column + head_dim))
                q_buf[index, span, :] = q_ref[source]
                product = do_buf[index, span, :].astype(F32) * o_ref[source].astype(F32)
                delta_ref[index, :, span] = jnp.sum(product.T, axis=0, keepdims=True)

    def load(s, kv, k_half, q_half):
        columns = slice(kv * head_dim, (kv + 1) * head_dim)
        span = pl.ds(pl.multiple_of(k_half * half, half), half)
        index = q_half * kv_heads + kv
        k = k_buf[s, span, columns]
        v = v_buf[s, span, columns]
        q = q_buf[index]
        do = do_buf[index]
        return (
            project_back(k, q), project_back(v, do), k, q, do, lse_ref[index], delta_ref[index]
        )

    def unit(loaded, mask=None):
        scores, d_probs, k, q, do, lse, delta = loaded
        probs = jnp.exp2(scores * factor - lse)
        if mask is not None:
            probs = jnp.where(mask, probs, 0.0)
        d_scores = (probs * (d_probs - delta)).astype(BF16)
        d_value = dot_nn(probs.astype(BF16), do)
        return dot_nn(d_scores, q), d_value, dot_nn(k.T, d_scores)

    group = 2 * half
    kv_width = kv_heads * head_dim

    def store(out_ref, index, p, kv, d_key, d_value):
        column = kv * head_dim
        span = pl.ds(pl.multiple_of(index * group + p * half, half), half)
        out_ref[span, column : column + head_dim] = d_key.astype(BF16)
        out_ref[span, kv_width + column : kv_width + column + head_dim] = d_value.astype(BF16)

    mask = causal_mask(info_ref, half, repeat, rows)
    wait_pieces(copies, True)
    for kv in range(kv_heads):
        dk_high, dv_high, dq = unit(load(0, kv, high, high), mask)
        acc_b[high * kv_heads + kv] = dq
        store(keep_ref, 0, high, kv, dk_high * scale, dv_high)
        dk_low, dv_low, dq = unit(load(0, kv, low, low), mask)
        acc_b[low * kv_heads + kv] = dq
        dk_more, dv_more, dq = unit(load(0, kv, low, high))
        acc_a[kv] = dq
        store(keep_ref, 0, low, kv, (dk_low + dk_more) * scale, dv_low + dv_more)
    wait_pieces(copies, False)

    def step(s, carry):
        earlier = info_ref[2 + s] < own_block
        chosen = jnp.where(earlier, low, high)
        keep = jnp.where(earlier, 1.0, 0.0)
        loaded = []
        for kv in range(kv_heads):
            loaded.append(load(s, kv, low, high))
            loaded.append(load(s, kv, chosen, chosen))
        units = [unit(item) for item in loaded]
        for kv in range(kv_heads):
            index = chosen * kv_heads + kv
            dq_a, dq_b = units[2 * kv][2], units[2 * kv + 1][2]
            acc_a[kv] = acc_a[kv] + dq_a
            acc_b[index] = acc_b[index] + dq_b

        def write(out_ref):
            index = lax.div(s, 2)
            for kv in range(kv_heads):
                dk_low, dv_low, _ = units[2 * kv]
                dk_sel, dv_sel, _ = units[2 * kv + 1]
                rest = 1.0 - keep
                store(
                    out_ref, index, low, kv, (dk_low + dk_sel * keep) * scale, dv_low + dv_sel * keep
                )
                store(out_ref, index, high, kv, dk_sel * (rest * scale), dv_sel * rest)

        odd = lax.rem(s, 2) == 1
        pl.when(odd)(lambda: write(send_ref))
        pl.when(jnp.logical_not(odd))(lambda: write(keep_ref))
        return carry

    lax.fori_loop(1, slots, step, 0)

    def finish(p, kv, values):
        span = pl.ds(pl.multiple_of(p * half, half), half)
        for r in range(repeat):
            column = (kv * repeat + r) * head_dim
            dq_ref[span, column : column + head_dim] = (
                values[:, r * half : (r + 1) * half].T * scale
            )

    for kv in range(kv_heads):
        finish(low, kv, acc_b[low * kv_heads + kv])
        finish(high, kv, acc_b[high * kv_heads + kv] + acc_a[kv])


def attention_backward(
    info, queries, attended, lse, output_weight, d_residual_slots, keys, values, head_dim
):
    slots = len(keys)
    shards = len(d_residual_slots)
    group_rows, width = queries.shape
    kv_width = keys[0].shape[1]
    kv_heads = kv_width // head_dim
    repeat = width // kv_width
    half = group_rows // 2
    wide = repeat * half
    piece = shape((slots // 2 * group_rows, 2 * kv_width), BF16)
    model = output_weight.shape[1]
    return pl.pallas_call(
        functools.partial(attention_backward_kernel, slots, shards, kv_heads, repeat),
        out_shape=(
            shape((group_rows, width), F32), piece, piece, shape((group_rows, model), BF16)
        ),
        in_specs=[SMEM_SPEC] + [VMEM_SPEC] * (4 + shards) + [ANY_SPEC] * (2 * slots),
        out_specs=(VMEM_SPEC,) * 4,
        scratch_shapes=[
            pltpu.VMEM((slots, group_rows, kv_width), BF16),
            pltpu.VMEM((slots, group_rows, kv_width), BF16),
            pltpu.VMEM((2 * kv_heads, wide, head_dim), BF16),
            pltpu.VMEM((2 * kv_heads, wide, head_dim), BF16),
            pltpu.VMEM((2 * kv_heads, 1, wide), F32),
            pltpu.VMEM((kv_heads, head_dim, wide), F32),
            pltpu.VMEM((2 * kv_heads, head_dim, wide), F32),
            pltpu.SemaphoreType.DMA((2, slots)),
        ],
        compiler_params=PARAMS,
        name="ab",
    )(
        info, queries, attended, lse, output_weight, *d_residual_slots, *keys, *values
    )


def body(
    layer_input,
    out_cotangent,
    block_map,
    first_gain,
    query_weight,
    key_weight,
    value_weight,
    query_gain,
    key_gain,
    output_weight,
    second_gain,
    gate_weight,
    up_weight,
    down_weight,
):
    groups = lax.axis_size("ctx")
    shards = lax.axis_size("tp")
    ctx_index = lax.axis_index("ctx")
    tp_index = lax.axis_index("tp")
    bits = list(range(1, groups.bit_length() - 1))
    head_dim = query_gain.shape[0]
    rows = layer_input.shape[0]
    group_rows = rows * shards
    half = group_rows // 2

    local = jnp.arange(group_rows, dtype=jnp.int32)
    within = jnp.bitwise_xor(local // rows, tp_index) * rows + local % rows
    own_block = lax.dynamic_index_in_dim(block_map, ctx_index, keepdims=False)
    block = jnp.where(within < half, own_block, 2 * groups - 1 - own_block)
    positions = block * half + within % half
    slot_blocks = jnp.take(block_map, jnp.bitwise_xor(jnp.arange(groups), ctx_index), axis=0)
    info = jnp.concatenate(
        [
            jnp.stack([tp_index // (shards // 2), tp_index % (shards // 2)]).astype(jnp.int32),
            slot_blocks.astype(jnp.int32),
        ]
    )

    x_slots = gather_slots(layer_input, "tp")
    cosine, sine = rope_tables(positions, head_dim)
    normed_a, key_linear, key_rows, value_rows = key_value(
        x_slots, first_gain, key_weight, value_weight, key_gain, cosine, sine
    )
    keys, values = gather_ctx(key_rows, value_rows, bits)
    cotangent_slots = gather_slots(after(out_cotangent, *x_slots), "tp")
    query_linear, queries = query_side(normed_a, query_weight, query_gain, cosine, sine)
    attended, lse, *attention_parts = attention_forward(
        info, queries, output_weight, keys, values, head_dim, shards
    )
    inputs_float = layer_input.astype(F32)
    residual = inputs_float + scatter_slots(attention_parts, "tp")
    normed_second, second_pull = jax.vjp(rms_apply, residual, second_gain)
    normed_slots = gather_slots(normed_second.astype(BF16), "tp")
    normed_b, cotangent_all, hidden, d_gate, d_upward, *second_parts = mlp_side(
        normed_slots, cotangent_slots, gate_weight, up_weight, down_weight
    )
    mlp_keep, mlp_send = weight_grads(
        ctx_index,
        groups,
        ((0, (0, 1)), (1, (2,))),
        (normed_b, cotangent_all),
        (d_gate, d_upward, hidden),
    )
    feedforward_parts = feedforward(hidden, down_weight, shards)
    d_second = scatter_slots(second_parts, "tp")
    mlp_own, mlp_got = exchange_ctx(mlp_keep, mlp_send)
    d_residual_norm, second_gain_part = second_pull(d_second)
    d_residual = out_cotangent.astype(F32) + d_residual_norm
    d_residual_slots = gather_slots(d_residual.astype(BF16), "tp")
    dq, dkv_keep, dkv_send, d_residual_all = attention_backward(
        info, queries, attended, lse, output_weight, d_residual_slots, keys, values, head_dim
    )
    dkv_own, dkv_got = exchange_ctx(dkv_keep, dkv_send)
    d_query_b, query_term, query_gain_part = query_backward(
        dq, query_linear, query_weight, query_gain, cosine, sine
    )
    feedforward_parts = after(tuple(feedforward_parts), dq)
    feedforward_part = scatter_slots(feedforward_parts, "tp")
    units = d_gate.shape[1]
    mlp_total = total_of(mlp_own, mlp_got)
    gate_sum, upward_sum = mlp_total[:, :units], mlp_total[:, units : 2 * units]
    down_sum = mlp_total[:, 2 * units :].T
    dkv_got, (gate_sum, upward_sum, down_sum) = hold(dkv_got, gate_sum, upward_sum, down_sum)
    query_keep, query_send = weight_grads(
        ctx_index, groups, ((0, (0,)), (1, (1,))), (d_residual_all, normed_a), (attended, d_query_b)
    )
    d_key_b, d_value_b, *first_parts = first_side(
        dkv_own,
        dkv_got,
        key_linear,
        key_weight,
        value_weight,
        key_gain,
        cosine,
        sine,
        query_term,
        normed_a,
        second_gain_part,
        query_gain_part,
        shards,
    )
    d_first = scatter_slots(first_parts, "tp")
    gains = sum_ctx(d_first[rows : rows + 3])
    d_first = d_first[:rows]
    key_keep, key_send = weight_grads(
        ctx_index, groups, ((0, (0, 1)),), (normed_a,), (d_key_b, d_value_b)
    )
    d_first = scatter_slots(first_parts, "tp")
    gains = sum_ctx(d_first[rows : rows + 3])
    d_first = d_first[:rows]
    key_keep, key_send = weight_grads(
        ctx_index, groups, ((0, (0, 1)),), (normed_a,), (d_key_b, d_value_b)
    )
    query_own, query_got = exchange_ctx(query_keep, query_send)
    key_own, key_got = exchange_ctx(key_keep, key_send)
    first_pull = jax.vjp(lambda v: rms_apply(v, first_gain), inputs_float)[1]
    input_grad = d_residual + first_pull(d_first)[0]

    layer_output = residual + feedforward_part
    query_total = total_of(query_own, query_got)
    key_total = total_of(key_own, key_got)
    query_width, key_width = attended.shape[1], d_key_b.shape[1]
    output_sum, query_sum = query_total[:, :query_width], query_total[:, query_width:]
    key_sum, value_sum = key_total[:, :key_width], key_total[:, key_width:]
    return (
        layer_output,
        input_grad,
        gains[0] / first_gain,
        query_sum,
        key_sum,
        value_sum,
        gains[2, :head_dim],
        gains[2, head_dim : 2 * head_dim],
        output_sum.T,
        gains[1],
        gate_sum,
        upward_sum,
        down_sum,
    )


def solution(mesh):
    return jax.shard_map(
        body,
        mesh=mesh,
        in_specs=(
            P(("ctx", "tp"), None),
            P(("ctx", "tp"), None),
            P(),
            P(),
            P(None, "tp"),
            P(None, "tp"),
            P(None, "tp"),
            P(),
            P(),
            P("tp", None),
            P(),
            P(None, "tp"),
            P(None, "tp"),
            P("tp", None),
        ),
        out_specs=(
            P(("ctx", "tp"), None),
            P(("ctx", "tp"), None),
            P(),
            P("ctx", "tp"),
            P("ctx", "tp"),
            P("ctx", "tp"),
            P(),
            P(),
            P("tp", "ctx"),
            P(),
            P("ctx", "tp"),
            P("ctx", "tp"),
            P("tp", "ctx"),
        ),
        check_vma=False,
    )
```
